32 devices in a mesh: mom: 4 (over y, core), pair: 8 (over z, x).
Axes of the slice: x: 2, y: 2, z: 4, core: 2. Of those that a mesh axis runs over, the one named last changes fastest.
Arguments:
- blocks: bfloat16 [4, 16, 1024, 1024], P('mom', None, 'pair'), may hold values from -1.078125 to 1.078125
- left_ids: int32 [4, 24], P('mom', 'pair'), may hold values from 0 to 15
- right_ids: int32 [4, 24], P('mom', 'pair'), may hold values from 0 to 15
- slice_ids: int32 [4, 24], P('mom', 'pair'), may hold values from 0 to 1
- weight_ids: int32 [4, 24], P('mom', 'pair'), may hold values from 0 to 7
- counts: int32 [4, 8], P('mom', 'pair'), may hold values from 1 to 3, 16 in all within a row
- subduction: float32 [8], replicated, may hold values from -1 to 1
Outputs:
- operator: float32 [4, 1024, 2, 1024], P('mom', 'pair')
The draws below stay inside these ranges and needn't reach their ends.
Inputs may be any that keep to these rules, and one draw needn't show every extreme that they name: Each row of counts sums to exactly 16.
All inputs are finite; a program needn't handle non-finite values. No bound on the sum of `counts` on one device may be relied on, other than what follows from the above.
Results may differ from the reference program's by a relative error of at most 0.0029.
Values may be sent and summed in bfloat16 or wider, within the bound.
No kernel may reach another device: no remote copies, remote signals or barrier semaphores. Data moves between devices by JAX's collectives and lax.ppermute only.
A program may use at most 128 MiB of HBM per device.

```python
import math
import jax
import jax.numpy as jnp
import numpy as np
from jax import lax

ORDER = 1024
FAM = 16
PAIR_DEV = 3
SLICES = 2
NW = 8
MOMS = 4
LISTS = 8
PAIRS = 24


def set_ends(values, rng, smallest, high):
    longest = values.shape.index(max(values.shape))
    spots = []
    for shift in (0, 1):
        where = [jax.random.randint(jax.random.fold_in(rng, axis), (), 0, length) for axis, length in enumerate(values.shape)]
        where[longest] = (where[longest] + shift) % values.shape[longest]
        spots.append(tuple(where))
    return values.at[spots[0]].set(smallest).at[spots[1]].set(high)


def block_levels(key, extent, split, least, top_value):
    def one(dim, blocks):
        steps = jax.random.uniform(jax.random.fold_in(jax.random.fold_in(key, 6), dim), (blocks,), jnp.float32, least / len(split), top_value / len(split))
        return jnp.repeat(jnp.exp(steps), extent[dim] // blocks).reshape((-1,) + (1,) * (len(extent) - dim - 1))

    gain = one(*split[0])
    for cut in split[1:]:
        gain = gain * one(*cut)
    return gain


def profile(number_of, total, bound, slope):
    loads = [(1 << 20) // math.isqrt(rank ** slope) + 1 for rank in range(2, number_of + 1)]
    spare, holding = total - bound - (number_of - 1), [1] * (number_of - 1)
    while spare > 0:
        movable = [i for i in range(number_of - 1) if holding[i] < bound]
        whole, left = sum([loads[i] for i in movable]), spare
        for i in movable:
            more = min(bound - holding[i], max(1, left * loads[i] // whole), spare)
            holding[i] = holding[i] + more
            spare = spare - more
    return np.array([bound] + holding)


def uneven(key, amount, total, bound, skew):
    if amount == 2:
        one = jax.random.randint(key, (), max(1, total - bound), min(bound, total - 1) + 1)
        return jnp.stack([one, total - one])
    lengths = jnp.asarray(profile(amount, total, bound, skew), jnp.int32)
    pairs = (amount - 1) // 2
    source_of, sink = lengths[1:1 + 2 * pairs:2], lengths[2:2 + 2 * pairs:2]
    room = jnp.minimum(source_of - 1, bound - sink)
    shifted = jax.random.randint(jax.random.fold_in(key, 1), (pairs,), 0, 1 << 20) % (room + 1)
    lengths = lengths.at[1:1 + 2 * pairs:2].set(source_of - shifted).at[2:2 + 2 * pairs:2].set(sink + shifted)
    return lengths[jax.random.permutation(jax.random.fold_in(key, 2), amount)]


def noise(stream_key, dims, spread, most, cuts=(), held_as=jnp.bfloat16):
    values = jax.random.normal(stream_key, dims, jnp.float32) * spread
    if len(cuts) > 0:
        values = block_levels(stream_key, dims, cuts, -0.22, 0.18) * values
    return jnp.clip(values, min=-most, max=most).astype(held_as)


def setup_inputs(seed: int = 0) -> dict:
    key_of = jax.random.split(jax.random.key(seed), 8)
    blocks = noise(key_of[0], (MOMS, FAM, ORDER, ORDER), 0.18, 1.078125, ((0, 4), (2, 8)))
    left_ids = set_ends(jax.random.randint(key_of[1], (MOMS, PAIRS), 0, FAM), jax.random.fold_in(key_of[1], 1), 0, FAM - 1).astype(jnp.int32)
    right_ids = set_ends(jax.random.randint(key_of[2], (MOMS, PAIRS), 0, FAM), jax.random.fold_in(key_of[2], 1), 0, FAM - 1).astype(jnp.int32)
    slice_ids = set_ends(jax.random.randint(key_of[3], (MOMS, PAIRS), 0, SLICES), jax.random.fold_in(key_of[3], 1), 0, SLICES - 1).astype(jnp.int32)
    weight_ids = set_ends(jax.random.randint(key_of[4], (MOMS, PAIRS), 0, NW), jax.random.fold_in(key_of[4], 1), 0, NW - 1).astype(jnp.int32)
    counts = jax.vmap(lambda own: uneven(own, LISTS, LISTS * (PAIR_DEV - 1), PAIR_DEV, 2))(jax.random.split(key_of[5], MOMS)).reshape((MOMS, LISTS)).astype(jnp.int32)
    subduction = jnp.clip(jax.random.uniform(key_of[6], (NW,), jnp.float32, -1.0, 1.0), -1.0, 1.0)
    return {"blocks": blocks, "left_ids": left_ids, "right_ids": right_ids, "slice_ids": slice_ids, "weight_ids": weight_ids, "counts": counts, "subduction": subduction}


def reference(blocks, left_ids, right_ids, slice_ids, weight_ids, counts, subduction):
    slot = jnp.arange(PAIRS, dtype=jnp.int32)
    fam_ids = jnp.arange(FAM, dtype=jnp.int32)
    outputs = []
    for family in range(MOMS):
        partner = family ^ 1
        limit = counts[family][slot // PAIR_DEV]
        live = (slot % PAIR_DEV) < limit
        weight = subduction[weight_ids[family]]
        select = (slice_ids[family][:, None] == jnp.arange(SLICES, dtype=jnp.int32)[None, :]).astype(jnp.float32)
        coef = jnp.where(live, weight, jnp.zeros_like(weight))[:, None] * select
        right_hot = (right_ids[family][:, None] == fam_ids[None, :]).astype(jnp.float32)
        left_hot = (left_ids[family][:, None] == fam_ids[None, :]).astype(jnp.float32)
        mixing = jnp.einsum("kt,kb,ka->tba", coef, right_hot, left_hot, precision=lax.Precision.HIGHEST)
        own = blocks[family].astype(jnp.float32).reshape(FAM, ORDER * ORDER)
        combined = jnp.dot(mixing.reshape(SLICES * FAM, FAM), own, precision=lax.Precision.HIGHEST)
        combined = combined.astype(jnp.bfloat16).reshape(SLICES, FAM, ORDER, ORDER)
        lefted = jnp.transpose(combined, (2, 0, 1, 3)).reshape(ORDER * SLICES, FAM * ORDER)
        total = jnp.dot(lefted, blocks[partner].reshape(FAM * ORDER, ORDER), preferred_element_type=jnp.float32)
        outputs.append(total.reshape(ORDER, SLICES, ORDER))
    return jnp.stack(outputs)
```

```python
import functools

import jax
import jax.numpy as jnp
from jax import lax
from jax.experimental import pallas as pl
from jax.experimental.pallas import tpu as pltpu
from jax.sharding import PartitionSpec as P

SLICES = 2
SUBLANES = 16
LANES = 128
PARTS = (3, 2, 2, 1)


def row_chunks(rows):
    units, total = rows // SUBLANES, sum(PARTS)
    edges = [0]
    for part in range(1, len(PARTS) + 1):
        edges.append(units * sum(PARTS[:part]) // total)
    return [
        (lo * SUBLANES, (hi - lo) * SUBLANES) for lo, hi in zip(edges, edges[1:]) if hi > lo
    ]


def swap(value, axis, apart):
    return lax.ppermute(value, axis, [(i, i ^ apart) for i in range(lax.axis_size(axis))])


def spec(space=pltpu.VMEM):
    return pl.BlockSpec(memory_space=space)


def plan_kernel(lists, families, *refs):
    metas, subduction = refs[:lists], refs[lists]
    left_list, weight_list, offsets, cursor = refs[lists + 1 :]
    keys = SLICES * families
    per_list = (metas[0].shape[1] - 1) // 4
    dump = lists * per_list

    def clear(q, carry):
        cursor[q] = 0
        return carry

    lax.fori_loop(0, keys + 1, clear, 0)
    slots = []
    for meta in metas:
        count = meta[0, 4 * per_list]
        for k in range(per_list):
            live = k < count
            key = meta[0, 2 * per_list + k] * families + meta[0, per_list + k]
            key = jnp.where(live, key, keys)
            slots.append((live, key, meta[0, k], meta[0, 3 * per_list + k]))
    for _, key, _, _ in slots:
        cursor[key] = cursor[key] + 1

    def place(q, total):
        here = cursor[q]
        offsets[q] = total
        cursor[q] = total
        return total + here

    offsets[keys] = lax.fori_loop(0, keys, place, 0)
    cursor[keys] = 0
    for live, key, left, weight in slots:
        at = cursor[key]
        cursor[key] = at + 1
        at = jnp.where(live, at, dump)
        left_list[at] = left
        weight_list[at] = subduction[weight]


def plan(metas, subduction, families):
    lists = len(metas)
    slots = lists * (metas[0].shape[1] - 1) // 4
    keys = SLICES * families
    return pl.pallas_call(
        functools.partial(plan_kernel, lists, families),
        out_shape=(
            jax.ShapeDtypeStruct((slots + 1,), jnp.int32),
            jax.ShapeDtypeStruct((slots + 1,), jnp.float32),
            jax.ShapeDtypeStruct((keys + 1,), jnp.int32),
        ),
        in_specs=[spec(pltpu.SMEM)] * (lists + 1),
        out_specs=(spec(pltpu.SMEM),) * 3,
        scratch_shapes=[pltpu.SMEM((keys + 1,), jnp.int32)],
        name="plan",
    )(*metas, subduction)


def pack_kernel(start, rows, width, me, own, *refs):
    outs, sems = refs[:-1], refs[-1]
    copies = []
    for offset, out in enumerate(outs):
        column = pl.multiple_of((me[0] ^ offset) * width, width)
        source = own.at[:, pl.ds(start, rows), pl.ds(column, width)]
        copies.append(pltpu.make_async_copy(source, out, sems.at[offset]))
    for copy in copies:
        copy.start()
    for copy in copies:
        copy.wait()


def pack(own, me, start, rows, width, devices):
    families = own.shape[0]
    if width % LANES:
        return [
            lax.dynamic_slice(
                own, (0, start, (me[0] ^ offset) * width), (families, rows, width)
            )
            for offset in range(devices)
        ]
    piece = jax.ShapeDtypeStruct((families, rows, width), own.dtype)
    return pl.pallas_call(
        functools.partial(pack_kernel, start, rows, width),
        out_shape=[piece] * devices,
        in_specs=[spec(pltpu.SMEM), spec(pl.ANY)],
        out_specs=[spec()] * devices,
        scratch_shapes=[pltpu.SemaphoreType.DMA((devices,))],
        cost_estimate=pl.CostEstimate(
            flops=0, transcendentals=0, bytes_accessed=4 * devices * piece.size
        ),
        name="pack",
    )(me, own)


def product_kernel(devices, left_list, weight_list, offsets, *refs):
    lefts, right = refs[:devices], refs[devices]
    send, keep, combined = refs[devices + 1 :]
    families, rows, width = lefts[0].shape
    order = right.shape[2]
    step = min(rows, 2 * SUBLANES)

    def combine(q, carry):
        t, b = q // families, q % families
        if isinstance(q, int):
            columns = pl.ds(b * width, width)
        else:
            columns = pl.ds(pl.multiple_of(b * width, width), width)
        first, last = offsets[q], offsets[q + 1]
        for top in range(0, rows, step):
            here = min(step, rows - top)

            def add(s, sums):
                left, weight = left_list[s], weight_list[s]
                return tuple(
                    total + weight * ref[left, top : top + here, :].astype(jnp.float32)
                    for total, ref in zip(sums, lefts)
                )

            zeros = (jnp.zeros((here, width), jnp.float32),) * devices
            sums = lax.fori_loop(first, last, add, zeros)
            for device, total in enumerate(sums):
                at = device * rows + top
                combined[t, at : at + here, columns] = total.astype(combined.dtype)
        return carry

    if width % LANES:
        for q in range(SLICES * families):
            combine(q, 0)
    else:
        lax.fori_loop(0, SLICES * families, combine, 0)

    tile = min(order, 2 * LANES)
    for t in range(SLICES):

        def multiply(i, carry):
            columns = pl.ds(pl.multiple_of(i * tile, tile), tile)
            target = pl.ds(pl.multiple_of(t * order + i * tile, tile), tile)
            part = jnp.dot(
                combined[t],
                right[:, :, columns].reshape(families * width, tile),
                preferred_element_type=jnp.float32,
            )
            for device in range(devices):
                piece = part[device * rows : (device + 1) * rows]
                if device % 2:
                    send[device // 2, :, target] = piece.astype(send.dtype)
                else:
                    keep[device // 2, :, target] = piece
            return carry

        lax.fori_loop(0, order // tile, multiply, 0)


def product(table, lefts, right):
    devices = len(lefts)
    families, rows, width = lefts[0].shape
    order = right.shape[2]
    shape = (devices // 2, rows, SLICES * order)
    depth = families * width
    return pl.pallas_call(
        functools.partial(product_kernel, devices),
        out_shape=(
            jax.ShapeDtypeStruct(shape, jnp.bfloat16),
            jax.ShapeDtypeStruct(shape, jnp.float32),
        ),
        in_specs=[spec(pltpu.SMEM)] * 3 + [spec()] * (devices + 1),
        out_specs=(spec(), spec()),
        scratch_shapes=[pltpu.VMEM((SLICES, devices * rows, depth), jnp.bfloat16)],
        compiler_params=pltpu.CompilerParams(vmem_limit_bytes=48 << 20),
        cost_estimate=pl.CostEstimate(
            flops=2 * SLICES * devices * rows * depth * order,
            transcendentals=0,
            bytes_accessed=2 * depth * (order + devices * rows) + 6 * devices * rows * order,
        ),
        name="product",
    )(*table, *lefts, right)


def halve_kernel(keep, came, send, kept):
    for i in range(send.shape[0]):
        kept[i] = keep[2 * i] + came[2 * i].astype(jnp.float32)
        total = keep[2 * i + 1] + came[2 * i + 1].astype(jnp.float32)
        send[i] = total.astype(send.dtype)


def halve(keep, came):
    shape = (keep.shape[0] // 2,) + keep.shape[1:]
    return pl.pallas_call(
        halve_kernel,
        out_shape=(
            jax.ShapeDtypeStruct(shape, jnp.bfloat16),
            jax.ShapeDtypeStruct(shape, jnp.float32),
        ),
        in_specs=[spec()] * 2,
        out_specs=(spec(), spec()),
        cost_estimate=pl.CostEstimate(
            flops=keep.size, transcendentals=0, bytes_accessed=9 * keep.size
        ),
        name="halve",
    )(keep, came)


def finish_kernel(start, order, keep, came, *refs):
    out, buffer, sem = refs[-3:]
    total = keep[0] + came[0].astype(jnp.float32)
    for t in range(SLICES):
        buffer[:, t, :] = total[:, t * order : (t + 1) * order]
    copy = pltpu.make_async_copy(buffer, out.at[pl.ds(start, buffer.shape[0])], sem)
    copy.start()
    copy.wait()


def finish(keep, came, start, rows, result):
    _, here, length = keep.shape
    order = length // SLICES
    before = [] if result is None else [result]
    return pl.pallas_call(
        functools.partial(finish_kernel, start, order),
        out_shape=jax.ShapeDtypeStruct((rows, SLICES, order), jnp.float32),
        in_specs=[spec()] * 2 + [spec(pl.ANY)] * len(before),
        out_specs=spec(pl.ANY),
        scratch_shapes=[
            pltpu.VMEM((here, SLICES, order), jnp.float32),
            pltpu.SemaphoreType.DMA,
        ],
        input_output_aliases={2: 0} if before else {},
        cost_estimate=pl.CostEstimate(
            flops=keep.size, transcendentals=0, bytes_accessed=10 * keep.size
        ),
        name="finish",
    )(keep, came, *before)


def body(blocks, left_ids, right_ids, slice_ids, weight_ids, counts, subduction):
    own = blocks[0]
    families, rows, order = own.shape
    devices = lax.axis_size("pair")
    width = order // devices
    me = lax.axis_index("pair").reshape(1)
    meta = jnp.concatenate([left_ids, right_ids, slice_ids, weight_ids, counts], axis=1)
    far_first = sorted(range(1, devices), reverse=True)
    metas = [meta] + [swap(meta, "pair", offset) for offset in far_first]
    chunks = row_chunks(rows)
    arrived = []
    for start, here in chunks:
        pieces = pack(own, me, start, here, width, devices)
        moved = {offset: swap(pieces[offset], "pair", offset) for offset in far_first}
        arrived.append([pieces[0]] + [moved[offset] for offset in range(1, devices)])
    right = swap(own, "mom", 1)
    table = plan(metas, subduction, families)
    result = None
    for (start, here), lefts in zip(chunks, arrived):
        send, keep = product(table, lefts, right)
        apart = 1
        while 2 * apart < devices:
            send, keep = halve(keep, swap(send, "pair", apart))
            apart *= 2
        result = finish(keep, swap(send, "pair", apart), start, rows, result)
    return result.reshape((1,) + result.shape)


def solution(mesh):
    return jax.shard_map(
        body,
        mesh=mesh,
        in_specs=(
            P("mom", None, "pair", None),
            P("mom", "pair"),
            P("mom", "pair"),
            P("mom", "pair"),
            P("mom", "pair"),
            P("mom", "pair"),
            P(),
        ),
        out_specs=P("mom", "pair", None, None),
        check_vma=False,
    )
```

```python
import functools

import jax
import jax.numpy as jnp
from jax import lax
from jax.experimental import pallas as pl
from jax.experimental.pallas import tpu as pltpu
from jax.sharding import PartitionSpec as P

SLICES = 2
SUBLANES = 16
LANES = 128
ROW_PARTS = (6, 2)
COLUMN_PARTS = (3, 1)


def cut(length, unit, parts):
    units, total = length // unit, sum(parts)
    edges = [units * sum(parts[:part]) // total for part in range(len(parts) + 1)]
    return [(lo * unit, (hi - lo) * unit) for lo, hi in zip(edges, edges[1:]) if hi > lo]


def swap(value, axis, apart):
    size = lax.axis_size(axis)
    return lax.ppermute(value, axis, [(i, i ^ apart) for i in range(size)])


def spec(space=pltpu.VMEM):
    return pl.BlockSpec(memory_space=space)


def plan_kernel(families, metas, subduction, left_list, weight_list, offsets, cursor):
    lists, keys = metas.shape[0], SLICES * families
    per_list = (metas.shape[1] - 1) // 4
    dump = lists * per_list

    def clear(q, carry):
        cursor[q] = 0
        return carry

    lax.fori_loop(0, keys + 1, clear, 0)
    slots = []
    for i in range(lists):
        count = metas[i, 4 * per_list]
        for k in range(per_list):
            live = k < count
            key = metas[i, 2 * per_list + k] * families + metas[i, per_list + k]
            key = jnp.where(live, key, keys)
            slots.append((live, key, metas[i, k], metas[i, 3 * per_list + k]))
    for _, key, _, _ in slots:
        cursor[key] = cursor[key] + 1

    def place(q, total):
        here = cursor[q]
        offsets[q] = total
        cursor[q] = total
        return total + here

    offsets[keys] = lax.fori_loop(0, keys, place, 0)
    cursor[keys] = 0
    for live, key, left, weight in slots:
        at = cursor[key]
        cursor[key] = at + 1
        at = jnp.where(live, at, dump)
        left_list[at] = left
        weight_list[at] = subduction[weight]


def plan(metas, subduction, families):
    slots = metas.shape[0] * (metas.shape[1] - 1) // 4
    keys = SLICES * families
    return pl.pallas_call(
        functools.partial(plan_kernel, families),
        out_shape=(
            jax.ShapeDtypeStruct((slots + 1,), jnp.int32),
            jax.ShapeDtypeStruct((slots + 1,), jnp.float32),
            jax.ShapeDtypeStruct((keys + 1,), jnp.int32),
        ),
        in_specs=[spec(pltpu.SMEM)] * 2,
        out_specs=(spec(pltpu.SMEM),) * 3,
        scratch_shapes=[pltpu.SMEM((keys + 1,), jnp.int32)],
        name="plan",
    )(metas, subduction)


def pack_kernel(start, rows, width, me, own, *refs):
    outs, sems = refs[:-1], refs[-1]
    copies = []
    for group, out in enumerate(outs):
        for half in range(2):
            column = pl.multiple_of((me[0] ^ (2 * group + half)) * width, width)
            source = own.at[:, pl.ds(start, rows), pl.ds(column, width)]
            sem = sems.at[2 * group + half]
            copies.append(pltpu.make_async_copy(source, out.at[half], sem))
    for copy in copies:
        copy.start()
    for copy in copies:
        copy.wait()


def pack(own, me, start, rows, width, groups):
    families = own.shape[0]
    if width % LANES:

        def columns(offset):
            at = (0, start, (me[0] ^ offset) * width)
            return lax.dynamic_slice(own, at, (families, rows, width))

        return [
            jnp.stack([columns(2 * group), columns(2 * group + 1)]) for group in range(groups)
        ]
    piece = jax.ShapeDtypeStruct((2, families, rows, width), own.dtype)
    return pl.pallas_call(
        functools.partial(pack_kernel, start, rows, width),
        out_shape=[piece] * groups,
        in_specs=[spec(pltpu.SMEM), spec(pl.ANY)],
        out_specs=[spec()] * groups,
        scratch_shapes=[pltpu.SemaphoreType.DMA((2 * groups,))],
        cost_estimate=pl.CostEstimate(
            flops=0, transcendentals=0, bytes_accessed=4 * groups * piece.size
        ),
        name="pack",
    )(me, own)


def slab_kernel(start, own, out, sem):
    copy = pltpu.make_async_copy(own.at[:, :, pl.ds(start, out.shape[2])], out, sem)
    copy.start()
    copy.wait()


def slab(own, start, columns):
    shape = own.shape[:2] + (columns,)
    return pl.pallas_call(
        functools.partial(slab_kernel, start),
        out_shape=jax.ShapeDtypeStruct(shape, own.dtype),
        in_specs=[spec(pl.ANY)],
        out_specs=spec(),
        scratch_shapes=[pltpu.SemaphoreType.DMA],
        cost_estimate=pl.CostEstimate(
            flops=0, transcendentals=0, bytes_accessed=4 * own.size * columns // own.shape[2]
        ),
        name="slab",
    )(own)


def combine_rows(table, lefts, combined):
    left_list, weight_list, offsets = table
    _, families, rows, width = lefts[0].shape
    step = min(rows, 2 * SUBLANES)

    def combine(q, carry):
        t, b = q // families, q % families
        first, last = offsets[q], offsets[q + 1]
        for top in range(0, rows, step):
            here = min(step, rows - top)

            def add(s, sums):
                left, weight = left_list[s], weight_list[s]
                pieces = [
                    ref[half, left, top : top + here, :].astype(jnp.float32)
                    for ref in lefts
                    for half in range(2)
                ]
                return tuple(total + weight * piece for total, piece in zip(sums, pieces))

            zeros = (jnp.zeros((here, width), jnp.float32),) * (2 * len(lefts))
            sums = lax.fori_loop(first, last, add, zeros)
            for i, total in enumerate(sums):
                at = (t * len(lefts) + i // 2) * rows + top
                start = (i % 2 * families + b) * width
                if not isinstance(q, int):
                    at = pl.multiple_of(at, SUBLANES)
                    start = pl.multiple_of(start, width)
                value = total.astype(combined.dtype)
                combined[pl.ds(at, here), pl.ds(start, width)] = value
        return carry

    if width % LANES:
        for q in range(SLICES * families):
            combine(q, 0)
    else:
        lax.fori_loop(0, SLICES * families, combine, 0)


def combine_kernel(*refs):
    combine_rows(refs[:3], refs[3:-1], refs[-1])


def combined_shape(lefts):
    _, families, rows, width = lefts[0].shape
    return SLICES * len(lefts) * rows, 2 * families * width


def combine(table, lefts):
    shape = combined_shape(lefts)
    size = shape[0] * shape[1]
    return pl.pallas_call(
        combine_kernel,
        out_shape=jax.ShapeDtypeStruct(shape, jnp.bfloat16),
        in_specs=[spec(pltpu.SMEM)] * 3 + [spec()] * len(lefts),
        out_specs=spec(),
        cost_estimate=pl.CostEstimate(
            flops=4 * size, transcendentals=0, bytes_accessed=3 * size
        ),
        name="combine",
    )(*table, *lefts)


def product_kernel(groups, chunks, edges, *refs):
    combined, near = refs[: len(chunks)], refs[len(chunks)]
    far, (send, keep) = refs[len(chunks) + 1 : -2], refs[-2:]
    families, width, tile = near.shape
    depth, step = families * width, pl.program_id(0)

    def multiply(other):
        top = 0
        for chunk in combined:
            part = jnp.dot(
                chunk[:, :depth],
                near[...].reshape(depth, tile),
                preferred_element_type=jnp.float32,
            ) + jnp.dot(
                chunk[:, depth:],
                other[...].reshape(depth, tile),
                preferred_element_type=jnp.float32,
            )
            rows = chunk.shape[0] // (SLICES * groups)
            for i in range(SLICES * groups):
                t, group = divmod(i, groups)
                piece = part[i * rows : (i + 1) * rows]
                if group % 2:
                    send[group // 2, t, top : top + rows] = piece.astype(send.dtype)
                else:
                    keep[group // 2, t, top : top + rows] = piece
            top += rows

    if len(far) == 1:
        multiply(far[0])
    else:
        for other, (lo, hi) in zip(far, edges):
            pl.when((step >= lo) & (step < hi))(functools.partial(multiply, other))


def product(combined, near, far, start, groups):
    families, width, _ = near.shape
    rows = [chunk.shape[0] // (SLICES * groups) for chunk in combined]
    columns = sum(part.shape[2] for part in far)
    tile = 2 * LANES
    edges, at = [], 0
    for part in far:
        edges.append((at, at + part.shape[2] // tile))
        at = edges[-1][1]

    def place(lo, hi):
        return lambda i: (0, 0, jnp.clip(i - lo, 0, hi - lo - 1))

    shape = (groups // 2, SLICES, sum(rows), columns)
    block = pl.BlockSpec((groups // 2, SLICES, sum(rows), tile), lambda i: (0, 0, 0, i))
    return pl.pallas_call(
        functools.partial(product_kernel, groups, rows, edges),
        grid=(columns // tile,),
        out_shape=(
            jax.ShapeDtypeStruct(shape, jnp.bfloat16),
            jax.ShapeDtypeStruct(shape, jnp.float32),
        ),
        in_specs=[
            pl.BlockSpec(chunk.shape, lambda i: (0, 0), pipeline_mode=pl.Buffered(1))
            for chunk in combined
        ]
        + [pl.BlockSpec((families, width, tile), lambda i: (0, 0, start // tile + i))]
        + [pl.BlockSpec((families, width, tile), place(lo, hi)) for lo, hi in edges],
        out_specs=(block, block),
        compiler_params=pltpu.CompilerParams(vmem_limit_bytes=48 << 20),
        cost_estimate=pl.CostEstimate(
            flops=2 * sum(chunk.size for chunk in combined) * columns,
            transcendentals=0,
            bytes_accessed=sum(2 * chunk.size for chunk in combined)
            + 4 * families * width * columns,
        ),
        name="product",
    )(*combined, near, *far)


def halve_kernel(keep, came, send, kept):
    for i in range(send.shape[0]):
        kept[i] = keep[2 * i] + came[2 * i].astype(jnp.float32)
        total = keep[2 * i + 1] + came[2 * i + 1].astype(jnp.float32)
        send[i] = total.astype(send.dtype)


def halve(keep, came):
    shape = (keep.shape[0] // 2,) + keep.shape[1:]
    return pl.pallas_call(
        halve_kernel,
        out_shape=(
            jax.ShapeDtypeStruct(shape, jnp.bfloat16),
            jax.ShapeDtypeStruct(shape, jnp.float32),
        ),
        in_specs=[spec()] * 2,
        out_specs=(spec(), spec()),
        cost_estimate=pl.CostEstimate(
            flops=keep.size, transcendentals=0, bytes_accessed=9 * keep.size
        ),
        name="halve",
    )(keep, came)


def finish_kernel(row, column, keep, came, *refs):
    out, buffer, sem = refs[-3:]
    rows, _, columns = buffer.shape
    for t in range(SLICES):
        buffer[:, t, :] = keep[0, t] + came[0, t].astype(jnp.float32)
    target = out.at[pl.ds(row, rows), :, pl.ds(column, columns)]
    copy = pltpu.make_async_copy(buffer, target, sem)
    copy.start()
    copy.wait()


def finish(keep, came, row, column, rows, order, result):
    here, columns = keep.shape[2:]
    before = [] if result is None else [result]
    return pl.pallas_call(
        functools.partial(finish_kernel, row, column),
        out_shape=jax.ShapeDtypeStruct((rows, SLICES, order), jnp.float32),
        in_specs=[spec()] * 2 + [spec(pl.ANY)] * len(before),
        out_specs=spec(pl.ANY),
        scratch_shapes=[
            pltpu.VMEM((here, SLICES, columns), jnp.float32),
            pltpu.SemaphoreType.DMA,
        ],
        input_output_aliases={2: 0} if before else {},
        cost_estimate=pl.CostEstimate(
            flops=keep.size, transcendentals=0, bytes_accessed=10 * keep.size
        ),
        name="finish",
    )(keep, came, *before)


def body(blocks, left_ids, right_ids, slice_ids, weight_ids, counts, subduction):
    own = blocks[0]
    families, rows, order = own.shape
    devices = lax.axis_size("pair")
    groups, width = devices // 2, order // devices
    me = lax.axis_index("pair").reshape(1)
    meta = jnp.concatenate([left_ids, right_ids, slice_ids, weight_ids, counts], axis=1)
    metas = lax.all_to_all(
        jnp.broadcast_to(meta, (devices, meta.shape[1])), "pair", 0, 0, tiled=True
    )
    row_cuts = cut(rows, SUBLANES, ROW_PARTS)
    column_cuts = cut(order, 2 * LANES, COLUMN_PARTS)
    arrived, far = [], []
    for i in range(max(len(row_cuts), len(column_cuts))):
        if i < len(row_cuts):
            pieces = pack(own, me, *row_cuts[i], width, groups)
            moved = [swap(pieces[group], "pair", 2 * group) for group in range(groups - 1, 0, -1)]
            arrived.append([pieces[0]] + moved[::-1])
        if i < len(column_cuts):
            part = own
            if len(column_cuts) > 1:
                part = slab(own, *column_cuts[i])
            far.append(swap(part, ("mom", "pair"), devices + 1))
    near = swap(own, "mom", 1)
    table = plan(metas, subduction, families)
    last, columns = len(row_cuts) - 1, range(len(column_cuts))
    jobs = [(range(last), [j]) for j in columns] + [([last], columns)]
    combined = [combine(table, lefts) for lefts in arrived]
    result = None
    for chunks, parts in jobs:
        row, column = row_cuts[chunks[0]][0], column_cuts[parts[0]][0]
        send, keep = product(
            [combined[i] for i in chunks], near, [far[j] for j in parts], column, groups
        )
        apart = 1
        while 2 * apart < groups:
            came = swap(send, "pair", 2 * apart)
            send, keep = halve(keep, came)
            apart *= 2
        came = swap(send, "pair", 2 * apart)
        result = finish(keep, came, row, column, rows, order, result)
    return result.reshape((1,) + result.shape)


def solution(mesh):
    return jax.shard_map(
        body,
        mesh=mesh,
        in_specs=(
            P("mom", None, "pair", None),
            P("mom", "pair"),
            P("mom", "pair"),
            P("mom", "pair"),
            P("mom", "pair"),
            P("mom", "pair"),
            P(),
        ),
        out_specs=P("mom", "pair", None, None),
        check_vma=False,
    )
```

```python
import functools

import jax
import jax.numpy as jnp
from jax import lax
from jax.experimental import pallas as pl
from jax.experimental.pallas import tpu as pltpu
from jax.sharding import PartitionSpec as P

SLICES = 2
SUBLANES = 16
LANES = 128
ROW_PARTS = (6, 2)
COLUMN_PARTS = (3, 1)


def cut(length, unit, parts):
    units, total = length // unit, sum(parts)
    edges = [units * sum(parts[:part]) // total for part in range(len(parts) + 1)]
    return [(lo * unit, (hi - lo) * unit) for lo, hi in zip(edges, edges[1:]) if hi > lo]


def swap(value, axis, apart):
    size = lax.axis_size(axis)
    return lax.ppermute(value, axis, [(i, i ^ apart) for i in range(size)])


def spec(space=pltpu.VMEM):
    return pl.BlockSpec(memory_space=space)


def base_count(families):
    return families - families // 4


def slot_fields(metas):
    per_list = (metas.shape[1] - 1) // 4
    for i in range(metas.shape[0]):
        count = metas[i, 4 * per_list]
        for k in range(per_list):
            yield (k < count,) + tuple(metas[i, field * per_list + k] for field in range(4))


def order_kernel(families, metas, left_order, left_rank, right_order, right_rank, more, used):
    def clear(a, carry):
        used[a] = 0
        used[families + 1 + a] = 0
        left_order[a] = 0
        right_order[a] = 0
        return carry

    lax.fori_loop(0, families + 1, clear, 0)
    for live, left, right, _, _ in slot_fields(metas):
        used[jnp.where(live, left, families)] = 1
        used[families + 1 + jnp.where(live, right, families)] = 1

    def place(a, found):
        lefts, rights = found
        left_rank[a] = lefts
        right_rank[a] = rights
        has_left, has_right = used[a], used[families + 1 + a]
        left_order[jnp.where(has_left > 0, lefts, families)] = a
        right_order[jnp.where(has_right > 0, rights, families)] = a
        return lefts + has_left, rights + has_right

    zero = jnp.int32(0)
    lefts, rights = lax.fori_loop(0, families, place, (zero, zero))
    more[0] = (jnp.maximum(lefts, rights) > base_count(families)).astype(jnp.int32)


def order_blocks(metas, families):
    ids = jax.ShapeDtypeStruct((families + 1,), jnp.int32)
    return pl.pallas_call(
        functools.partial(order_kernel, families),
        out_shape=(ids, ids, ids, ids, jax.ShapeDtypeStruct((1,), jnp.int32)),
        in_specs=[spec(pltpu.SMEM)],
        out_specs=(spec(pltpu.SMEM),) * 5,
        scratch_shapes=[pltpu.SMEM((2 * families + 2,), jnp.int32)],
        name="order",
    )(metas)


def plan_kernel(
    families, metas, left_rank, right_rank, subduction, left_list, weight_list, offsets, cursor
):
    base, keys = base_count(families), 2 * SLICES * families
    dump = left_list.shape[0] - 1

    def clear(q, carry):
        cursor[q] = 0
        return carry

    lax.fori_loop(0, keys + 1, clear, 0)
    slots = []
    for live, left, right, piece, weight in slot_fields(metas):
        rank = left_rank[left]
        late = (rank >= base).astype(jnp.int32)
        key = 2 * (piece * families + right_rank[right]) + late
        slots.append((live, jnp.where(live, key, keys), rank - base * late, weight))
    for _, key, _, _ in slots:
        cursor[key] = cursor[key] + 1

    def place(q, total):
        here = cursor[q]
        offsets[q] = total
        cursor[q] = total
        return total + here

    offsets[keys] = lax.fori_loop(0, keys, place, 0)
    cursor[keys] = 0
    for live, key, rank, weight in slots:
        at = cursor[key]
        cursor[key] = at + 1
        at = jnp.where(live, at, dump)
        left_list[at] = rank
        weight_list[at] = subduction[weight]


def plan(metas, left_rank, right_rank, subduction, families):
    slots = metas.shape[0] * (metas.shape[1] - 1) // 4
    keys = 2 * SLICES * families
    return pl.pallas_call(
        functools.partial(plan_kernel, families),
        out_shape=(
            jax.ShapeDtypeStruct((slots + 1,), jnp.int32),
            jax.ShapeDtypeStruct((slots + 1,), jnp.float32),
            jax.ShapeDtypeStruct((keys + 1,), jnp.int32),
        ),
        in_specs=[spec(pltpu.SMEM)] * 4,
        out_specs=(spec(pltpu.SMEM),) * 3,
        scratch_shapes=[pltpu.SMEM((keys + 1,), jnp.int32)],
        name="plan",
    )(metas, left_rank, right_rank, subduction)


def pack_kernel(first, start, rows, width, order, me, own, *refs):
    outs, sem = refs[:-1], refs[-1]
    copies = []
    for group, out in enumerate(outs):
        for half in range(2):
            column = pl.multiple_of((me[0] ^ (2 * group + half)) * width, width)
            for i in range(out.shape[1]):
                source = own.at[order[first + i], pl.ds(start, rows), pl.ds(column, width)]
                at = (2 * group + half) * out.shape[1] + i
                copies.append(pltpu.make_async_copy(source, out.at[half, i], sem.at[at]))
    for copy in copies:
        copy.start()
    for copy in copies:
        copy.wait()


def pack(own, order, me, first, number, start, rows, width, groups):
    if width % LANES:
        blocks = jnp.take(own, order[first : first + number], axis=0)

        def columns(offset):
            at = (0, start, (me[0] ^ offset) * width)
            return lax.dynamic_slice(blocks, at, (number, rows, width))

        return [
            jnp.stack([columns(2 * group), columns(2 * group + 1)]) for group in range(groups)
        ]
    piece = jax.ShapeDtypeStruct((2, number, rows, width), own.dtype)
    return pl.pallas_call(
        functools.partial(pack_kernel, first, start, rows, width),
        out_shape=[piece] * groups,
        in_specs=[spec(pltpu.SMEM)] * 2 + [spec(pl.ANY)],
        out_specs=[spec()] * groups,
        scratch_shapes=[pltpu.SemaphoreType.DMA((2 * groups * number,))],
        cost_estimate=pl.CostEstimate(
            flops=0, transcendentals=0, bytes_accessed=4 * groups * piece.size
        ),
        compiler_params=pltpu.CompilerParams(vmem_limit_bytes=8 << 20),
        name="pack",
    )(order, me, own)


def slab_kernel(first, start, order, own, out, sem):
    copies = []
    for i in range(out.shape[0]):
        source = own.at[order[first + i], :, pl.ds(start, out.shape[2])]
        copies.append(pltpu.make_async_copy(source, out.at[i], sem.at[i]))
    for copy in copies:
        copy.start()
    for copy in copies:
        copy.wait()


def slab(own, order, first, number, start, columns):
    shape = (number, own.shape[1], columns)
    return pl.pallas_call(
        functools.partial(slab_kernel, first, start),
        out_shape=jax.ShapeDtypeStruct(shape, own.dtype),
        in_specs=[spec(pltpu.SMEM), spec(pl.ANY)],
        out_specs=spec(),
        scratch_shapes=[pltpu.SemaphoreType.DMA((number,))],
        cost_estimate=pl.CostEstimate(
            flops=0, transcendentals=0, bytes_accessed=4 * number * own.shape[1] * columns
        ),
        compiler_params=pltpu.CompilerParams(vmem_limit_bytes=8 << 20),
        name="slab",
    )(order, own)


def unset(shapes):
    return pl.pallas_call(
        lambda *refs: None,
        out_shape=shapes,
        out_specs=[spec(pl.ANY)] * len(shapes),
        name="unset",
    )()


def late_blocks(own, left_order, right_order, me, more, width, groups):
    families, rows, order = own.shape
    devices, first = 2 * groups, base_count(families)
    number = families - first
    piece = jax.ShapeDtypeStruct((2, number, rows, width), own.dtype)
    part = jax.ShapeDtypeStruct((number, rows, order), own.dtype)

    def exchange():
        pieces = pack(own, left_order, me, first, number, 0, rows, width, groups)
        moved = [swap(pieces[group], "pair", 2 * group) for group in range(1, groups)]
        mine = slab(own, right_order, first, number, 0, order)
        near = swap(mine, "mom", 1)
        far = swap(mine, ("mom", "pair"), devices + 1)
        return [pieces[0], *moved, near, far]

    def skip():
        return list(unset([piece] * groups + [part] * 2))

    arrays = lax.cond(more, exchange, skip)
    return arrays[:groups], arrays[groups], arrays[groups + 1]


def combine_rows(table, more, lefts, lates, combined):
    left_list, weight_list, offsets = table
    _, base, rows, width = lefts[0].shape
    families = base + lates[0].shape[1]
    step = min(rows, 2 * SUBLANES)

    def combine(t, b):
        q = 2 * (t * families + b)
        for top in range(0, rows, step):
            here = min(step, rows - top)

            def add_from(refs, low):
                def add(s, sums):
                    left, weight = left_list[s], weight_list[s]
                    pieces = [
                        ref[half, left, low : low + here, :].astype(jnp.float32)
                        for ref in refs
                        for half in range(2)
                    ]
                    return tuple(total + weight * piece for total, piece in zip(sums, pieces))

                return add

            sums = (jnp.zeros((here, width), jnp.float32),) * (2 * len(lefts))
            sums = lax.fori_loop(offsets[q], offsets[q + 1], add_from(lefts, top), sums)
            sums = lax.fori_loop(
                offsets[q + 1], offsets[q + 2], add_from(lates, top), sums
            )
            for i, total in enumerate(sums):
                group, half = divmod(i, 2)
                at = (t * len(lefts) + group) * rows + top
                column = jnp.where(
                    b < base,
                    half * base + b,
                    2 * base + half * (families - base) + b - base,
                )
                if isinstance(b, int):
                    column = half * base + b
                    if b >= base:
                        column = 2 * base + half * (families - base) + b - base
                    column *= width
                else:
                    at = pl.multiple_of(at, SUBLANES)
                    column = pl.multiple_of(column * width, width)
                value = total.astype(combined.dtype)
                combined[pl.ds(at, here), pl.ds(column, width)] = value

    if width % LANES:
        for t in range(SLICES):
            for b in range(families):
                combine(t, b)
        return
    count = jnp.where(more[0] > 0, families, base)

    def both(b, carry):
        for t in range(SLICES):
            combine(t, b)
        return carry

    lax.fori_loop(0, count, both, 0)


def fetch_if(wanted, sources, targets, sems):
    @pl.when(wanted)
    def fetch():
        copies = [
            pltpu.make_async_copy(source, target, sems.at[i])
            for i, (source, target) in enumerate(zip(sources, targets))
        ]
        for copy in copies:
            copy.start()
        for copy in copies:
            copy.wait()


def combine_kernel(start, groups, *refs):
    table, more, refs = refs[:3], refs[3], refs[4:]
    lefts, lates, combined = refs[:groups], refs[groups : 2 * groups], refs[2 * groups]
    held, sems = refs[2 * groups + 1 : -1], refs[-1]
    rows = lefts[0].shape[2]
    sources = [late.at[:, :, pl.ds(start, rows)] for late in lates]
    fetch_if(more[0] > 0, sources, held, sems)
    combine_rows(table, more, lefts, held, combined)


def combine(table, more, lefts, lates, start):
    _, base, rows, width = lefts[0].shape
    families = base + lates[0].shape[1]
    shape = SLICES * len(lefts) * rows, 2 * families * width
    size = shape[0] * shape[1]
    return pl.pallas_call(
        functools.partial(combine_kernel, start, len(lefts)),
        out_shape=jax.ShapeDtypeStruct(shape, jnp.bfloat16),
        in_specs=[spec(pltpu.SMEM)] * 4
        + [spec()] * len(lefts)
        + [spec(pl.ANY)] * len(lates),
        out_specs=spec(),
        scratch_shapes=[pltpu.VMEM((2, families - base, rows, width), jnp.bfloat16)] * len(lates)
        + [pltpu.SemaphoreType.DMA((len(lates),))],
        compiler_params=pltpu.CompilerParams(vmem_limit_bytes=20 << 20),
        cost_estimate=pl.CostEstimate(
            flops=4 * size, transcendentals=0, bytes_accessed=3 * size
        ),
        name="combine",
    )(*table, more, *lefts, *lates)


def product_kernel(groups, chunks, edges, start, more, *refs):
    combined, refs = refs[: len(chunks)], refs[len(chunks) :]
    nears, fars, refs = refs[: len(edges)], refs[len(edges) : 2 * len(edges)], refs[-7:]
    lates, (send, keep), held, sems = refs[:2], refs[2:4], refs[4:6], refs[6]
    _, width, tile = nears[0].shape
    step = pl.program_id(0)
    columns = pl.ds(pl.multiple_of(start + step * tile, tile), tile)
    fetch_if(more[0] > 0, [late.at[:, :, columns] for late in lates], held, sems)

    def multiply(parts):
        top = 0
        for chunk in combined:
            total, at = None, 0
            for part in parts:
                depth = part.shape[0] * width
                term = jnp.dot(
                    chunk[:, at : at + depth],
                    part[...].reshape(depth, tile),
                    preferred_element_type=jnp.float32,
                )
                total = term if total is None else total + term
                at += depth
            rows = chunk.shape[0] // (SLICES * groups)
            for i in range(SLICES * groups):
                t, group = divmod(i, groups)
                piece = total[i * rows : (i + 1) * rows]
                if group % 2:
                    send[group // 2, t, top : top + rows] = piece.astype(send.dtype)
                else:
                    keep[group // 2, t, top : top + rows] = piece
            top += rows

    for near, far, (lo, hi) in zip(nears, fars, edges):
        here = (step >= lo) & (step < hi)
        usual = functools.partial(multiply, (near, far))
        full = functools.partial(multiply, (near, far, *held))
        pl.when(here & (more[0] == 0))(usual)
        pl.when(here & (more[0] > 0))(full)


def product(more, combined, nears, fars, lates, start, groups):
    base, width, _ = nears[0].shape
    late = lates[0].shape[0]
    rows = [chunk.shape[0] // (SLICES * groups) for chunk in combined]
    columns = sum(part.shape[2] for part in fars)
    tile = 2 * LANES
    edges, at = [], 0
    for part in fars:
        edges.append((at, at + part.shape[2] // tile))
        at = edges[-1][1]

    def place(lo, hi):
        return lambda i: (0, 0, jnp.clip(i - lo, 0, hi - lo - 1))

    shape = (groups // 2, SLICES, sum(rows), columns)
    block = pl.BlockSpec((groups // 2, SLICES, sum(rows), tile), lambda i: (0, 0, 0, i))
    return pl.pallas_call(
        functools.partial(product_kernel, groups, rows, edges, start),
        grid=(columns // tile,),
        out_shape=(
            jax.ShapeDtypeStruct(shape, jnp.bfloat16),
            jax.ShapeDtypeStruct(shape, jnp.float32),
        ),
        in_specs=[spec(pltpu.SMEM)]
        + [
            pl.BlockSpec(chunk.shape, lambda i: (0, 0), pipeline_mode=pl.Buffered(1))
            for chunk in combined
        ]
        + [pl.BlockSpec((base, width, tile), place(lo, hi)) for lo, hi in edges] * 2
        + [spec(pl.ANY)] * 2,
        out_specs=(block, block),
        scratch_shapes=[pltpu.VMEM((late, width, tile), jnp.bfloat16)] * 2
        + [pltpu.SemaphoreType.DMA((2,))],
        compiler_params=pltpu.CompilerParams(vmem_limit_bytes=24 << 20),
        cost_estimate=pl.CostEstimate(
            flops=2 * sum(chunk.size for chunk in combined) * columns,
            transcendentals=0,
            bytes_accessed=sum(2 * chunk.size for chunk in combined)
            + 4 * (base + late) * width * columns,
        ),
        name="product",
    )(more, *combined, *nears, *fars, *lates)


def halve_kernel(keep, came, send, kept):
    for i in range(send.shape[0]):
        kept[i] = keep[2 * i] + came[2 * i].astype(jnp.float32)
        total = keep[2 * i + 1] + came[2 * i + 1].astype(jnp.float32)
        send[i] = total.astype(send.dtype)


def halve(keep, came):
    shape = (keep.shape[0] // 2,) + keep.shape[1:]
    return pl.pallas_call(
        halve_kernel,
        out_shape=(
            jax.ShapeDtypeStruct(shape, jnp.bfloat16),
            jax.ShapeDtypeStruct(shape, jnp.float32),
        ),
        in_specs=[spec()] * 2,
        out_specs=(spec(), spec()),
        cost_estimate=pl.CostEstimate(
            flops=keep.size, transcendentals=0, bytes_accessed=9 * keep.size
        ),
        compiler_params=pltpu.CompilerParams(vmem_limit_bytes=8 << 20),
        name="halve",
    )(keep, came)


def finish_kernel(row, column, keep, came, *refs):
    out, buffer, sem = refs[-3:]
    rows, _, columns = buffer.shape
    for t in range(SLICES):
        buffer[:, t, :] = keep[0, t] + came[0, t].astype(jnp.float32)
    target = out.at[pl.ds(row, rows), :, pl.ds(column, columns)]
    copy = pltpu.make_async_copy(buffer, target, sem)
    copy.start()
    copy.wait()


def finish(keep, came, row, column, rows, order, result):
    here, columns = keep.shape[2:]
    before = [] if result is None else [result]
    return pl.pallas_call(
        functools.partial(finish_kernel, row, column),
        out_shape=jax.ShapeDtypeStruct((rows, SLICES, order), jnp.float32),
        in_specs=[spec()] * 2 + [spec(pl.ANY)] * len(before),
        out_specs=spec(pl.ANY),
        scratch_shapes=[
            pltpu.VMEM((here, SLICES, columns), jnp.float32),
            pltpu.SemaphoreType.DMA,
        ],
        input_output_aliases={2: 0} if before else {},
        cost_estimate=pl.CostEstimate(
            flops=keep.size, transcendentals=0, bytes_accessed=10 * keep.size
        ),
        compiler_params=pltpu.CompilerParams(vmem_limit_bytes=8 << 20),
        name="finish",
    )(keep, came, *before)


def body(blocks, left_ids, right_ids, slice_ids, weight_ids, counts, subduction):
    own = blocks[0]
    families, rows, order = own.shape
    devices = lax.axis_size("pair")
    groups, width = devices // 2, order // devices
    me = lax.axis_index("pair").reshape(1)
    meta = jnp.concatenate([left_ids, right_ids, slice_ids, weight_ids, counts], axis=1)
    metas = lax.all_to_all(
        jnp.broadcast_to(meta, (devices, meta.shape[1])), "pair", 0, 0, tiled=True
    )
    partner = swap(metas, "mom", 1)
    left_order, left_rank, _, right_rank, more = order_blocks(metas, families)
    right_order = order_blocks(partner, families)[2]
    base = base_count(families)
    row_cuts = cut(rows, SUBLANES, ROW_PARTS)
    column_cuts = cut(order, 2 * LANES, COLUMN_PARTS)
    arrived, nears, fars = [], [], []
    for start, here in row_cuts:
        pieces = pack(
            own, left_order, me, 0, base, start, here, width, groups
        )
        moved = [swap(pieces[group], "pair", 2 * group) for group in range(groups - 1, 0, -1)]
        arrived.append([pieces[0]] + moved[::-1])
    for start, columns in column_cuts:
        mine = slab(own, right_order, 0, base, start, columns)
        fars.append(swap(mine, ("mom", "pair"), devices + 1))
        nears.append(swap(mine, "mom", 1))
    anywhere = more
    for bit in range(lax.axis_size("mom").bit_length() - 1):
        anywhere = jnp.maximum(anywhere, swap(anywhere, "mom", 1 << bit))
    late_lefts, late_near, late_far = late_blocks(
        own, left_order, right_order, me, anywhere[0] > 0, width, groups
    )
    table = plan(metas, left_rank, right_rank, subduction, families)
    last, columns = len(row_cuts) - 1, range(len(column_cuts))
    jobs = [(range(last), [j]) for j in columns] + [([last], columns)]
    combined = [
        combine(table, more, lefts, late_lefts, row_cuts[i][0])
        for i, lefts in enumerate(arrived)
    ]
    result = None
    for chunks, parts in jobs:
        row, column = row_cuts[chunks[0]][0], column_cuts[parts[0]][0]
        send, keep = product(
            more,
            [combined[i] for i in chunks],
            [nears[j] for j in parts],
            [fars[j] for j in parts],
            [late_near, late_far],
            column,
            groups,
        )
        apart = 1
        while 2 * apart < groups:
            came = swap(send, "pair", 2 * apart)
            send, keep = halve(keep, came)
            apart *= 2
        came = swap(send, "pair", 2 * apart)
        result = finish(keep, came, row, column, rows, order, result)
    return result.reshape((1,) + result.shape)


def solution(mesh):
    return jax.shard_map(
        body,
        mesh=mesh,
        in_specs=(
            P("mom", None, "pair", None),
            P("mom", "pair"),
            P("mom", "pair"),
            P("mom", "pair"),
            P("mom", "pair"),
            P("mom", "pair"),
            P(),
        ),
        out_specs=P("mom", "pair", None, None),
        check_vma=False,
    )
```

```python
import functools

import jax
import jax.numpy as jnp
from jax import lax
from jax.experimental import pallas as pl
from jax.experimental.pallas import tpu as pltpu
from jax.sharding import PartitionSpec as P

SLICES = 2
SUBLANES = 16
LANES = 128
ROW_PARTS = (1, 5, 2)
COLUMN_PARTS = (1, 2, 1)
HALVES = (True, True, False)


def cut(length, unit, parts):
    units, total = length // unit, sum(parts)
    edges = [units * sum(parts[:part]) // total for part in range(len(parts) + 1)]
    return [(lo * unit, (hi - lo) * unit) for lo, hi in zip(edges, edges[1:]) if hi > lo]


def swap(value, axis, apart):
    size = lax.axis_size(axis)
    return lax.ppermute(value, axis, [(i, i ^ apart) for i in range(size)])


def spec(space=pltpu.VMEM):
    return pl.BlockSpec(memory_space=space)


def base_count(families):
    return families - 3 * families // 16


def slot_fields(metas):
    per_list = (metas.shape[1] - 1) // 4
    for i in range(metas.shape[0]):
        count = metas[i, 4 * per_list]
        for k in range(per_list):
            yield (k < count,) + tuple(metas[i, field * per_list + k] for field in range(4))


def order_kernel(families, metas, left_order, left_rank, right_order, right_rank, more, used):
    def clear(a, carry):
        used[a] = 0
        used[families + 1 + a] = 0
        left_order[a] = 0
        right_order[a] = 0
        return carry

    lax.fori_loop(0, families + 1, clear, 0)
    for live, left, right, _, _ in slot_fields(metas):
        used[jnp.where(live, left, families)] = 1
        used[families + 1 + jnp.where(live, right, families)] = 1

    def place(a, found):
        lefts, rights = found
        left_rank[a] = lefts
        right_rank[a] = rights
        has_left, has_right = used[a], used[families + 1 + a]
        left_order[jnp.where(has_left > 0, lefts, families)] = a
        right_order[jnp.where(has_right > 0, rights, families)] = a
        return lefts + has_left, rights + has_right

    zero = jnp.int32(0)
    lefts, rights = lax.fori_loop(0, families, place, (zero, zero))
    more[0] = (jnp.maximum(lefts, rights) > base_count(families)).astype(jnp.int32)


def order_blocks(metas, families):
    ids = jax.ShapeDtypeStruct((families + 1,), jnp.int32)
    return pl.pallas_call(
        functools.partial(order_kernel, families),
        out_shape=(ids, ids, ids, ids, jax.ShapeDtypeStruct((1,), jnp.int32)),
        in_specs=[spec(pltpu.SMEM)],
        out_specs=(spec(pltpu.SMEM),) * 5,
        scratch_shapes=[pltpu.SMEM((2 * families + 2,), jnp.int32)],
        name="order",
    )(metas)


def plan_kernel(
    families, metas, left_rank, right_rank, subduction, left_list, weight_list, offsets, cursor
):
    base, keys = base_count(families), 2 * SLICES * families
    dump = left_list.shape[0] - 1

    def clear(q, carry):
        cursor[q] = 0
        return carry

    lax.fori_loop(0, keys + 1, clear, 0)
    slots = []
    for live, left, right, piece, weight in slot_fields(metas):
        rank = left_rank[left]
        late = (rank >= base).astype(jnp.int32)
        key = 2 * (piece * families + right_rank[right]) + late
        slots.append((live, jnp.where(live, key, keys), rank - base * late, weight))
    for _, key, _, _ in slots:
        cursor[key] = cursor[key] + 1

    def place(q, total):
        here = cursor[q]
        offsets[q] = total
        cursor[q] = total
        return total + here

    offsets[keys] = lax.fori_loop(0, keys, place, 0)
    cursor[keys] = 0
    for live, key, rank, weight in slots:
        at = cursor[key]
        cursor[key] = at + 1
        at = jnp.where(live, at, dump)
        left_list[at] = rank
        weight_list[at] = subduction[weight]


def plan(metas, left_rank, right_rank, subduction, families):
    slots = metas.shape[0] * (metas.shape[1] - 1) // 4
    keys = 2 * SLICES * families
    return pl.pallas_call(
        functools.partial(plan_kernel, families),
        out_shape=(
            jax.ShapeDtypeStruct((slots + 1,), jnp.int32),
            jax.ShapeDtypeStruct((slots + 1,), jnp.float32),
            jax.ShapeDtypeStruct((keys + 1,), jnp.int32),
        ),
        in_specs=[spec(pltpu.SMEM)] * 4,
        out_specs=(spec(pltpu.SMEM),) * 3,
        scratch_shapes=[pltpu.SMEM((keys + 1,), jnp.int32)],
        name="plan",
    )(metas, left_rank, right_rank, subduction)


def pack_kernel(first, start, rows, width, *refs):
    order, refs = (None, refs) if first is None else (refs[0], refs[1:])
    me, own, outs, sem = refs[0], refs[1], refs[2:-1], refs[-1]
    copies = []
    for group, out in enumerate(outs):
        for half in range(2):
            column = pl.multiple_of((me[0] ^ (2 * group + half)) * width, width)
            if order is None:
                source = own.at[:, pl.ds(start, rows), pl.ds(column, width)]
                at = sem.at[2 * group + half]
                copies.append(pltpu.make_async_copy(source, out.at[half], at))
                continue
            for i in range(out.shape[1]):
                source = own.at[order[first + i], pl.ds(start, rows), pl.ds(column, width)]
                at = (2 * group + half) * out.shape[1] + i
                copies.append(pltpu.make_async_copy(source, out.at[half, i], sem.at[at]))
    for copy in copies:
        copy.start()
    for copy in copies:
        copy.wait()


def pack(own, order, me, first, number, start, rows, width, groups):
    if width % LANES:
        blocks = own
        if order is not None:
            blocks = jnp.take(own, order[first : first + number], axis=0)

        def columns(offset):
            at = (0, start, (me[0] ^ offset) * width)
            return lax.dynamic_slice(blocks, at, (number, rows, width))

        return [
            jnp.stack([columns(2 * group), columns(2 * group + 1)]) for group in range(groups)
        ]
    piece = jax.ShapeDtypeStruct((2, number, rows, width), own.dtype)
    orders = [] if order is None else [order]
    return pl.pallas_call(
        functools.partial(pack_kernel, first if orders else None, start, rows, width),
        out_shape=[piece] * groups,
        in_specs=[spec(pltpu.SMEM)] * (1 + len(orders)) + [spec(pl.ANY)],
        out_specs=[spec()] * groups,
        scratch_shapes=[pltpu.SemaphoreType.DMA((2 * groups * number,))],
        cost_estimate=pl.CostEstimate(
            flops=0, transcendentals=0, bytes_accessed=4 * groups * piece.size
        ),
        compiler_params=pltpu.CompilerParams(vmem_limit_bytes=8 << 20),
        name="pack",
    )(*orders, me, own)


def slab_kernel(first, start, *refs):
    own, out, sem = refs[-3:]
    if first is None:
        whole = own.at[:, :, pl.ds(start, out.shape[2])]
        copy = pltpu.make_async_copy(whole, out, sem.at[0])
        copy.start()
        copy.wait()
        return
    order, copies = refs[0], []
    for i in range(out.shape[0]):
        source = own.at[order[first + i], :, pl.ds(start, out.shape[2])]
        copies.append(pltpu.make_async_copy(source, out.at[i], sem.at[i]))
    for copy in copies:
        copy.start()
    for copy in copies:
        copy.wait()


def slab(own, order, first, number, start, columns):
    shape = (number, own.shape[1], columns)
    orders = [] if order is None else [order]
    return pl.pallas_call(
        functools.partial(slab_kernel, first if orders else None, start),
        out_shape=jax.ShapeDtypeStruct(shape, own.dtype),
        in_specs=[spec(pltpu.SMEM)] * len(orders) + [spec(pl.ANY)],
        out_specs=spec(),
        scratch_shapes=[pltpu.SemaphoreType.DMA((number,))],
        cost_estimate=pl.CostEstimate(
            flops=0, transcendentals=0, bytes_accessed=4 * number * own.shape[1] * columns
        ),
        compiler_params=pltpu.CompilerParams(vmem_limit_bytes=8 << 20),
        name="slab",
    )(*orders, own)


def pick_kernel(order, *refs):
    count = len(refs) // 2
    whole, outs, sem = refs[:count], refs[count:-1], refs[-1]
    number = outs[0].shape[1]
    copies = []
    for j, (source, out) in enumerate(zip(whole, outs)):
        for i in range(number):
            piece = source.at[:, pl.ds(order[i], 1)]
            copies.append(
                pltpu.make_async_copy(piece, out.at[:, pl.ds(i, 1)], sem.at[j * number + i])
            )
    for copy in copies:
        copy.start()
    for copy in copies:
        copy.wait()


def pick(order, number, *whole):
    shapes = [
        jax.ShapeDtypeStruct((piece.shape[0], number) + piece.shape[2:], piece.dtype)
        for piece in whole
    ]
    return pl.pallas_call(
        pick_kernel,
        out_shape=shapes,
        in_specs=[spec(pltpu.SMEM)] + [spec(pl.ANY)] * len(whole),
        out_specs=[spec()] * len(whole),
        scratch_shapes=[pltpu.SemaphoreType.DMA((number * len(whole),))],
        compiler_params=pltpu.CompilerParams(vmem_limit_bytes=8 << 20),
        cost_estimate=pl.CostEstimate(
            flops=0, transcendentals=0, bytes_accessed=4 * sum(piece.size for piece in whole)
        ),
        name="pick",
    )(order, *whole)


def unset(shapes):
    return pl.pallas_call(
        lambda *refs: None,
        out_shape=shapes,
        out_specs=[spec(pl.ANY)] * len(shapes),
        name="unset",
    )()


def late_blocks(own, left_order, right_order, me, more, width, groups):
    families, rows, order = own.shape
    devices, first = 2 * groups, base_count(families)
    number = families - first
    piece = jax.ShapeDtypeStruct((2, number, rows, width), own.dtype)
    part = jax.ShapeDtypeStruct((number, rows, order), own.dtype)

    def exchange():
        pieces = pack(own, left_order, me, first, number, 0, rows, width, groups)
        moved = [swap(pieces[group], "pair", 2 * group) for group in range(1, groups)]
        mine = slab(own, right_order, first, number, 0, order)
        near = swap(mine, "mom", 1)
        far = swap(mine, ("mom", "pair"), devices + 1)
        return [pieces[0], *moved, near, far]

    def skip():
        return list(unset([piece] * groups + [part] * 2))

    arrays = lax.cond(more, exchange, skip)
    return arrays[:groups], arrays[groups], arrays[groups + 1]


def combine_rows(table, more, lefts, lates, combined):
    left_list, weight_list, offsets = table
    _, base, rows, width = lefts[0].shape
    families = base + lates[0].shape[1]
    step = min(rows, 2 * SUBLANES)

    def combine(t, b):
        q = 2 * (t * families + b)
        for top in range(0, rows, step):
            here = min(step, rows - top)

            def add_from(refs, low):
                def add(s, sums):
                    left, weight = left_list[s], weight_list[s]
                    pieces = [
                        ref[half, left, low : low + here, :].astype(jnp.float32)
                        for ref in refs
                        for half in range(2)
                    ]
                    return tuple(total + weight * piece for total, piece in zip(sums, pieces))

                return add

            sums = (jnp.zeros((here, width), jnp.float32),) * (2 * len(lefts))
            sums = lax.fori_loop(offsets[q], offsets[q + 1], add_from(lefts, top), sums)
            sums = lax.fori_loop(
                offsets[q + 1], offsets[q + 2], add_from(lates, top), sums
            )
            for i, total in enumerate(sums):
                group, half = divmod(i, 2)
                at = (t * len(lefts) + group) * rows + top
                column = jnp.where(
                    b < base,
                    half * base + b,
                    2 * base + half * (families - base) + b - base,
                )
                if isinstance(b, int):
                    column = half * base + b
                    if b >= base:
                        column = 2 * base + half * (families - base) + b - base
                    column *= width
                else:
                    at = pl.multiple_of(at, SUBLANES)
                    column = pl.multiple_of(column * width, width)
                value = total.astype(combined.dtype)
                combined[pl.ds(at, here), pl.ds(column, width)] = value

    if width % LANES:
        for t in range(SLICES):
            for b in range(families):
                combine(t, b)
        return
    count = jnp.where(more[0] > 0, families, base)

    def both(b, carry):
        for t in range(SLICES):
            combine(t, b)
        return carry

    lax.fori_loop(0, count, both, 0)


def fetch_if(wanted, sources, targets, sems):
    @pl.when(wanted)
    def fetch():
        copies = [
            pltpu.make_async_copy(source, target, sems.at[i])
            for i, (source, target) in enumerate(zip(sources, targets))
        ]
        for copy in copies:
            copy.start()
        for copy in copies:
            copy.wait()


def combine_kernel(start, groups, *refs):
    table, more, refs = refs[:3], refs[3], refs[4:]
    lefts, lates, combined = refs[:groups], refs[groups : 2 * groups], refs[2 * groups]
    held, sems = refs[2 * groups + 1 : -1], refs[-1]
    rows = lefts[0].shape[2]
    sources = [late.at[:, :, pl.ds(start, rows)] for late in lates]
    fetch_if(more[0] > 0, sources, held, sems)
    combine_rows(table, more, lefts, held, combined)


def combine(table, more, lefts, lates, start):
    _, base, rows, width = lefts[0].shape
    families = base + lates[0].shape[1]
    shape = SLICES * len(lefts) * rows, 2 * families * width
    size = shape[0] * shape[1]
    return pl.pallas_call(
        functools.partial(combine_kernel, start, len(lefts)),
        out_shape=jax.ShapeDtypeStruct(shape, jnp.bfloat16),
        in_specs=[spec(pltpu.SMEM)] * 4
        + [spec()] * len(lefts)
        + [spec(pl.ANY)] * len(lates),
        out_specs=spec(),
        scratch_shapes=[pltpu.VMEM((2, families - base, rows, width), jnp.bfloat16)] * len(lates)
        + [pltpu.SemaphoreType.DMA((len(lates),))],
        compiler_params=pltpu.CompilerParams(vmem_limit_bytes=20 << 20),
        cost_estimate=pl.CostEstimate(
            flops=4 * size, transcendentals=0, bytes_accessed=3 * size
        ),
        name="combine",
    )(*table, more, *lefts, *lates)


def product_kernel(groups, chunks, edges, start, halves, more, *refs):
    combined, refs = refs[: len(chunks)], refs[len(chunks) :]
    nears, fars, refs = refs[: len(edges)], refs[len(edges) : 2 * len(edges)], refs[2 * len(edges) :]
    lates, outs, held, sems = refs[:2], refs[2:-3], refs[-3:-1], refs[-1]
    _, width, tile = nears[0].shape
    step = pl.program_id(0)
    columns = pl.ds(pl.multiple_of(start + step * tile, tile), tile)
    fetch_if(more[0] > 0, [late.at[:, :, columns] for late in lates], held, sems)

    def multiply(parts):
        top = 0
        for chunk in combined:
            total, at = None, 0
            for part in parts:
                depth = part.shape[0] * width
                term = jnp.dot(
                    chunk[:, at : at + depth],
                    part[...].reshape(depth, tile),
                    preferred_element_type=jnp.float32,
                )
                total = term if total is None else total + term
                at += depth
            rows = chunk.shape[0] // (SLICES * groups)
            for i in range(SLICES * groups):
                t, group = divmod(i, groups)
                piece = total[i * rows : (i + 1) * rows]
                if halves:
                    out, at = outs[1 - group % 2], group // 2
                else:
                    out, at = outs[group - 1], 0
                out[at, t, top : top + rows] = piece.astype(out.dtype)
            top += rows

    for near, far, (lo, hi) in zip(nears, fars, edges):
        here = (step >= lo) & (step < hi)
        usual = functools.partial(multiply, (near, far))
        full = functools.partial(multiply, (near, far, *held))
        pl.when(here & (more[0] == 0))(usual)
        pl.when(here & (more[0] > 0))(full)


def product(halves, more, combined, nears, fars, lates, start, groups):
    base, width, _ = nears[0].shape
    late = lates[0].shape[0]
    rows = [chunk.shape[0] // (SLICES * groups) for chunk in combined]
    columns = sum(part.shape[2] for part in fars)
    tile = 2 * LANES
    edges, at = [], 0
    for part in fars:
        edges.append((at, at + part.shape[2] // tile))
        at = edges[-1][1]

    def place(lo, hi):
        return lambda i: (0, 0, jnp.clip(i - lo, 0, hi - lo - 1))

    kept, sends = (groups // 2, 1) if halves else (1, groups - 1)
    shape = (kept, SLICES, sum(rows), columns)
    block = pl.BlockSpec((kept, SLICES, sum(rows), tile), lambda i: (0, 0, 0, i))
    return pl.pallas_call(
        functools.partial(product_kernel, groups, rows, edges, start, halves),
        grid=(columns // tile,),
        out_shape=[jax.ShapeDtypeStruct(shape, jnp.bfloat16)] * sends
        + [jax.ShapeDtypeStruct(shape, jnp.float32)],
        in_specs=[spec(pltpu.SMEM)]
        + [
            pl.BlockSpec(chunk.shape, lambda i: (0, 0), pipeline_mode=pl.Buffered(1))
            for chunk in combined
        ]
        + [pl.BlockSpec((base, width, tile), place(lo, hi)) for lo, hi in edges] * 2
        + [spec(pl.ANY)] * 2,
        out_specs=[block] * (sends + 1),
        scratch_shapes=[pltpu.VMEM((late, width, tile), jnp.bfloat16)] * 2
        + [pltpu.SemaphoreType.DMA((2,))],
        compiler_params=pltpu.CompilerParams(vmem_limit_bytes=24 << 20),
        cost_estimate=pl.CostEstimate(
            flops=2 * sum(chunk.size for chunk in combined) * columns,
            transcendentals=0,
            bytes_accessed=sum(2 * chunk.size for chunk in combined)
            + 4 * (base + late) * width * columns,
        ),
        name="product",
    )(more, *combined, *nears, *fars, *lates)


def halve_kernel(keep, came, send, kept):
    for i in range(send.shape[0]):
        kept[i] = keep[2 * i] + came[2 * i].astype(jnp.float32)
        total = keep[2 * i + 1] + came[2 * i + 1].astype(jnp.float32)
        send[i] = total.astype(send.dtype)


def halve(keep, came):
    shape = (keep.shape[0] // 2,) + keep.shape[1:]
    return pl.pallas_call(
        halve_kernel,
        out_shape=(
            jax.ShapeDtypeStruct(shape, jnp.bfloat16),
            jax.ShapeDtypeStruct(shape, jnp.float32),
        ),
        in_specs=[spec()] * 2,
        out_specs=(spec(), spec()),
        cost_estimate=pl.CostEstimate(
            flops=keep.size, transcendentals=0, bytes_accessed=9 * keep.size
        ),
        compiler_params=pltpu.CompilerParams(vmem_limit_bytes=8 << 20),
        name="halve",
    )(keep, came)


def finish_kernel(row, column, count, keep, *refs):
    cames, (out, buffer, sem) = refs[:count], refs[-3:]
    rows, _, columns = buffer.shape
    for t in range(SLICES):
        total = keep[0, t]
        for came in cames:
            total = total + came[0, t].astype(jnp.float32)
        buffer[:, t, :] = total
    target = out.at[pl.ds(row, rows), :, pl.ds(column, columns)]
    copy = pltpu.make_async_copy(buffer, target, sem)
    copy.start()
    copy.wait()


def finish(keep, cames, row, column, rows, order, result):
    here, columns = keep.shape[2:]
    before = [] if result is None else [result]
    return pl.pallas_call(
        functools.partial(finish_kernel, row, column, len(cames)),
        out_shape=jax.ShapeDtypeStruct((rows, SLICES, order), jnp.float32),
        in_specs=[spec()] * (1 + len(cames)) + [spec(pl.ANY)] * len(before),
        out_specs=spec(pl.ANY),
        scratch_shapes=[
            pltpu.VMEM((here, SLICES, columns), jnp.float32),
            pltpu.SemaphoreType.DMA,
        ],
        input_output_aliases={1 + len(cames): 0} if before else {},
        cost_estimate=pl.CostEstimate(
            flops=keep.size, transcendentals=0, bytes_accessed=10 * keep.size
        ),
        compiler_params=pltpu.CompilerParams(vmem_limit_bytes=8 << 20),
        name="finish",
    )(keep, *cames, *before)


def body(blocks, left_ids, right_ids, slice_ids, weight_ids, counts, subduction):
    own = blocks[0]
    families, rows, order = own.shape
    devices = lax.axis_size("pair")
    groups, width = devices // 2, order // devices
    me = lax.axis_index("pair").reshape(1)
    meta = jnp.concatenate([left_ids, right_ids, slice_ids, weight_ids, counts], axis=1)
    metas = lax.all_to_all(
        jnp.broadcast_to(meta, (devices, meta.shape[1])), "pair", 0, 0, tiled=True
    )
    partner = swap(metas, "mom", 1)
    left_order, left_rank, needed, right_rank, more = order_blocks(metas, families)
    right_order = order_blocks(partner, families)[2]
    base = base_count(families)
    row_cuts = cut(rows, SUBLANES, ROW_PARTS)
    column_cuts = cut(order, 2 * LANES, COLUMN_PARTS)
    arrived, nears, fars = [], [], []
    for i, (start, here) in enumerate(row_cuts):
        chosen, number = (left_order, base) if i else (None, families)
        pieces = pack(
            own, chosen, me, 0, number, start, here, width, groups
        )
        moved = [swap(pieces[group], "pair", 2 * group) for group in range(groups - 1, 0, -1)]
        pieces = [pieces[0]] + moved[::-1]
        if not i:
            pieces = list(pick(left_order, base, *pieces))
        arrived.append(pieces)
    for i, (start, columns) in enumerate(column_cuts):
        chosen, number = (right_order, base) if i else (None, families)
        mine = slab(own, chosen, 0, number, start, columns)
        far = swap(mine, ("mom", "pair"), devices + 1)
        near = swap(mine, "mom", 1)
        if not i:
            near, far = pick(needed, base, near[None], far[None])
            near, far = near[0], far[0]
        fars.append(far)
        nears.append(near)
    anywhere = more
    for bit in range(lax.axis_size("mom").bit_length() - 1):
        anywhere = jnp.maximum(anywhere, swap(anywhere, "mom", 1 << bit))
    late_lefts, late_near, late_far = late_blocks(
        own, left_order, right_order, me, anywhere[0] > 0, width, groups
    )
    table = plan(metas, left_rank, right_rank, subduction, families)
    last, columns = len(row_cuts) - 1, range(len(column_cuts))
    jobs = [(range(last), columns[:-1]), (range(last), columns[-1:]), ([last], columns)]
    combined = [
        combine(table, more, lefts, late_lefts, row_cuts[i][0])
        for i, lefts in enumerate(arrived)
    ]
    result = None
    for k, (chunks, parts) in enumerate(jobs):
        row, column = row_cuts[chunks[0]][0], column_cuts[parts[0]][0]
        halves = HALVES[k]
        *sends, keep = functools.partial(product, halves)(
            more,
            [combined[i] for i in chunks],
            [nears[j] for j in parts],
            [fars[j] for j in parts],
            [late_near, late_far],
            column,
            groups,
        )
        apart, steps = 1, [0] * (groups.bit_length() - 2) if halves else []
        for _ in steps:
            came = swap(sends[0], "pair", 2 * apart)
            *sends, keep = halve(keep, came)
            apart *= 2
        if halves:
            cames = [swap(sends[0], "pair", 2 * apart)]
        else:
            cames = [
                swap(sends[group - 1], "pair", 2 * group)
                for group in range(groups - 1, 0, -1)
            ]
        result = finish(keep, cames, row, column, rows, order, result)
    return result.reshape((1,) + result.shape)


def solution(mesh):
    return jax.shard_map(
        body,
        mesh=mesh,
        in_specs=(
            P("mom", None, "pair", None),
            P("mom", "pair"),
            P("mom", "pair"),
            P("mom", "pair"),
            P("mom", "pair"),
            P("mom", "pair"),
            P(),
        ),
        out_specs=P("mom", "pair", None, None),
        check_vma=False,
    )
```

```python
import functools

import jax
import jax.numpy as jnp
from jax import lax
from jax.experimental import pallas as pl
from jax.experimental.pallas import tpu as pltpu
from jax.sharding import PartitionSpec as P

SLICES = 2
SUBLANES = 16
LANES = 128
ROW_PARTS = (1, 5, 2)
COLUMN_PARTS = (1, 2, 1)
HALVES = (True, True, False)


def cut(length, unit, parts):
    units, total = length // unit, sum(parts)
    edges = [units * sum(parts[:part]) // total for part in range(len(parts) + 1)]
    return [(lo * unit, (hi - lo) * unit) for lo, hi in zip(edges, edges[1:]) if hi > lo]


def swap(value, axis, apart):
    size = lax.axis_size(axis)
    return lax.ppermute(value, axis, [(i, i ^ apart) for i in range(size)])


def spec(space=pltpu.VMEM):
    return pl.BlockSpec(memory_space=space)


def base_count(families):
    return families - 3 * families // 16


def slot_fields(metas):
    per_list = (metas.shape[1] - 1) // 4
    for i in range(metas.shape[0]):
        count = metas[i, 4 * per_list]
        for k in range(per_list):
            yield (k < count,) + tuple(metas[i, field * per_list + k] for field in range(4))


def order_kernel(families, metas, left_order, left_rank, right_order, right_rank, more, used):
    def clear(a, carry):
        used[a] = 0
        used[families + 1 + a] = 0
        left_order[a] = 0
        right_order[a] = 0
        return carry

    lax.fori_loop(0, families + 1, clear, 0)
    for live, left, right, _, _ in slot_fields(metas):
        used[jnp.where(live, left, families)] = 1
        used[families + 1 + jnp.where(live, right, families)] = 1

    def place(a, found):
        lefts, rights = found
        left_rank[a] = lefts
        right_rank[a] = rights
        has_left, has_right = used[a], used[families + 1 + a]
        left_order[jnp.where(has_left > 0, lefts, families)] = a
        right_order[jnp.where(has_right > 0, rights, families)] = a
        return lefts + has_left, rights + has_right

    zero = jnp.int32(0)
    lefts, rights = lax.fori_loop(0, families, place, (zero, zero))
    more[0] = (jnp.maximum(lefts, rights) > base_count(families)).astype(jnp.int32)


def order_blocks(metas, families):
    ids = jax.ShapeDtypeStruct((families + 1,), jnp.int32)
    return pl.pallas_call(
        functools.partial(order_kernel, families),
        out_shape=(ids, ids, ids, ids, jax.ShapeDtypeStruct((1,), jnp.int32)),
        in_specs=[spec(pltpu.SMEM)],
        out_specs=(spec(pltpu.SMEM),) * 5,
        scratch_shapes=[pltpu.SMEM((2 * families + 2,), jnp.int32)],
        name="order",
    )(metas)


def plan_kernel(
    families, metas, left_rank, right_rank, subduction, left_list, weight_list, offsets, cursor
):
    base, keys = base_count(families), 2 * SLICES * families
    dump = left_list.shape[0] - 1

    def clear(q, carry):
        cursor[q] = 0
        return carry

    lax.fori_loop(0, keys + 1, clear, 0)
    slots = []
    for live, left, right, piece, weight in slot_fields(metas):
        rank = left_rank[left]
        late = (rank >= base).astype(jnp.int32)
        key = 2 * (piece * families + right_rank[right]) + late
        slots.append((live, jnp.where(live, key, keys), rank - base * late, weight))
    for _, key, _, _ in slots:
        cursor[key] = cursor[key] + 1

    def place(q, total):
        here = cursor[q]
        offsets[q] = total
        cursor[q] = total
        return total + here

    offsets[keys] = lax.fori_loop(0, keys, place, 0)
    cursor[keys] = 0
    for live, key, rank, weight in slots:
        at = cursor[key]
        cursor[key] = at + 1
        at = jnp.where(live, at, dump)
        left_list[at] = rank
        weight_list[at] = subduction[weight]


def plan(metas, left_rank, right_rank, subduction, families):
    slots = metas.shape[0] * (metas.shape[1] - 1) // 4
    keys = 2 * SLICES * families
    return pl.pallas_call(
        functools.partial(plan_kernel, families),
        out_shape=(
            jax.ShapeDtypeStruct((slots + 1,), jnp.int32),
            jax.ShapeDtypeStruct((slots + 1,), jnp.float32),
            jax.ShapeDtypeStruct((keys + 1,), jnp.int32),
        ),
        in_specs=[spec(pltpu.SMEM)] * 4,
        out_specs=(spec(pltpu.SMEM),) * 3,
        scratch_shapes=[pltpu.SMEM((keys + 1,), jnp.int32)],
        name="plan",
    )(metas, left_rank, right_rank, subduction)


def pack_kernel(first, start, rows, width, *refs):
    order, refs = (None, refs) if first is None else (refs[0], refs[1:])
    me, own, outs, sem = refs[0], refs[1], refs[2:-1], refs[-1]
    copies = []
    for group, out in enumerate(outs):
        for half in range(2):
            column = pl.multiple_of((me[0] ^ (2 * group + half)) * width, width)
            if order is None:
                source = own.at[:, pl.ds(start, rows), pl.ds(column, width)]
                at = sem.at[2 * group + half]
                copies.append(pltpu.make_async_copy(source, out.at[half], at))
                continue
            for i in range(out.shape[1]):
                source = own.at[order[first + i], pl.ds(start, rows), pl.ds(column, width)]
                at = (2 * group + half) * out.shape[1] + i
                copies.append(pltpu.make_async_copy(source, out.at[half, i], sem.at[at]))
    for copy in copies:
        copy.start()
    for copy in copies:
        copy.wait()


def pack(own, order, me, first, number, start, rows, width, groups):
    if width % LANES:
        blocks = own
        if order is not None:
            blocks = jnp.take(own, order[first : first + number], axis=0)

        def columns(offset):
            at = (0, start, (me[0] ^ offset) * width)
            return lax.dynamic_slice(blocks, at, (number, rows, width))

        return [
            jnp.stack([columns(2 * group), columns(2 * group + 1)]) for group in range(groups)
        ]
    piece = jax.ShapeDtypeStruct((2, number, rows, width), own.dtype)
    orders = [] if order is None else [order]
    return pl.pallas_call(
        functools.partial(pack_kernel, first if orders else None, start, rows, width),
        out_shape=[piece] * groups,
        in_specs=[spec(pltpu.SMEM)] * (1 + len(orders)) + [spec(pl.ANY)],
        out_specs=[spec()] * groups,
        scratch_shapes=[pltpu.SemaphoreType.DMA((2 * groups * number,))],
        cost_estimate=pl.CostEstimate(
            flops=0, transcendentals=0, bytes_accessed=4 * groups * piece.size
        ),
        compiler_params=pltpu.CompilerParams(vmem_limit_bytes=6 << 20),
        name="pack",
    )(*orders, me, own)


def slab_kernel(first, start, *refs):
    own, out, sem = refs[-3:]
    if first is None:
        whole = own.at[:, :, pl.ds(start, out.shape[2])]
        copy = pltpu.make_async_copy(whole, out, sem.at[0])
        copy.start()
        copy.wait()
        return
    order, copies = refs[0], []
    for i in range(out.shape[0]):
        source = own.at[order[first + i], :, pl.ds(start, out.shape[2])]
        copies.append(pltpu.make_async_copy(source, out.at[i], sem.at[i]))
    for copy in copies:
        copy.start()
    for copy in copies:
        copy.wait()


def slab(own, order, first, number, start, columns):
    shape = (number, own.shape[1], columns)
    orders = [] if order is None else [order]
    return pl.pallas_call(
        functools.partial(slab_kernel, first if orders else None, start),
        out_shape=jax.ShapeDtypeStruct(shape, own.dtype),
        in_specs=[spec(pltpu.SMEM)] * len(orders) + [spec(pl.ANY)],
        out_specs=spec(),
        scratch_shapes=[pltpu.SemaphoreType.DMA((number,))],
        cost_estimate=pl.CostEstimate(
            flops=0, transcendentals=0, bytes_accessed=4 * number * own.shape[1] * columns
        ),
        compiler_params=pltpu.CompilerParams(vmem_limit_bytes=6 << 20),
        name="slab",
    )(*orders, own)


def pick_kernel(order, *refs):
    count = len(refs) // 2
    whole, outs, sem = refs[:count], refs[count:-1], refs[-1]
    number = outs[0].shape[1]
    copies = []
    for j, (source, out) in enumerate(zip(whole, outs)):
        for i in range(number):
            piece = source.at[:, pl.ds(order[i], 1)]
            copies.append(
                pltpu.make_async_copy(piece, out.at[:, pl.ds(i, 1)], sem.at[j * number + i])
            )
    for copy in copies:
        copy.start()
    for copy in copies:
        copy.wait()


def pick(order, number, *whole):
    shapes = [
        jax.ShapeDtypeStruct((piece.shape[0], number) + piece.shape[2:], piece.dtype)
        for piece in whole
    ]
    return pl.pallas_call(
        pick_kernel,
        out_shape=shapes,
        in_specs=[spec(pltpu.SMEM)] + [spec(pl.ANY)] * len(whole),
        out_specs=[spec()] * len(whole),
        scratch_shapes=[pltpu.SemaphoreType.DMA((number * len(whole),))],
        compiler_params=pltpu.CompilerParams(vmem_limit_bytes=6 << 20),
        cost_estimate=pl.CostEstimate(
            flops=0, transcendentals=0, bytes_accessed=4 * sum(piece.size for piece in whole)
        ),
        name="pick",
    )(order, *whole)


def unset(shapes):
    return pl.pallas_call(
        lambda *refs: None,
        out_shape=shapes,
        out_specs=[spec(pl.ANY)] * len(shapes),
        name="unset",
    )()


def late_blocks(own, left_order, right_order, me, more, width, groups):
    families, rows, order = own.shape
    devices, first = 2 * groups, base_count(families)
    number = families - first
    piece = jax.ShapeDtypeStruct((2, number, rows, width), own.dtype)
    part = jax.ShapeDtypeStruct((number, rows, order), own.dtype)

    def exchange():
        pieces = pack(own, left_order, me, first, number, 0, rows, width, groups)
        moved = [swap(pieces[group], "pair", 2 * group) for group in range(1, groups)]
        mine = slab(own, right_order, first, number, 0, order)
        near = swap(mine, "mom", 1)
        far = swap(mine, ("mom", "pair"), devices + 1)
        return [pieces[0], *moved, near, far]

    def skip():
        return list(unset([piece] * groups + [part] * 2))

    arrays = lax.cond(more, exchange, skip)
    return arrays[:groups], arrays[groups], arrays[groups + 1]


def combine_rows(table, more, lefts, lates, combined):
    left_list, weight_list, offsets = table
    _, base, rows, width = lefts[0].shape
    families = base + lates[0].shape[1]
    step = min(rows, 2 * SUBLANES)

    def combine(t, b):
        q = 2 * (t * families + b)
        for top in range(0, rows, step):
            here = min(step, rows - top)

            def add_from(refs, low):
                def add(s, sums):
                    left, weight = left_list[s], weight_list[s]
                    pieces = [
                        ref[half, left, low : low + here, :].astype(jnp.float32)
                        for ref in refs
                        for half in range(2)
                    ]
                    return tuple(total + weight * piece for total, piece in zip(sums, pieces))

                return add

            sums = (jnp.zeros((here, width), jnp.float32),) * (2 * len(lefts))
            sums = lax.fori_loop(offsets[q], offsets[q + 1], add_from(lefts, top), sums)
            sums = lax.fori_loop(
                offsets[q + 1], offsets[q + 2], add_from(lates, top), sums
            )
            for i, total in enumerate(sums):
                group, half = divmod(i, 2)
                at = (t * len(lefts) + group) * rows + top
                column = jnp.where(
                    b < base,
                    half * base + b,
                    2 * base + half * (families - base) + b - base,
                )
                if isinstance(b, int):
                    column = half * base + b
                    if b >= base:
                        column = 2 * base + half * (families - base) + b - base
                    column *= width
                else:
                    at = pl.multiple_of(at, SUBLANES)
                    column = pl.multiple_of(column * width, width)
                value = total.astype(combined.dtype)
                combined[pl.ds(at, here), pl.ds(column, width)] = value

    if width % LANES:
        for t in range(SLICES):
            for b in range(families):
                combine(t, b)
        return
    count = jnp.where(more[0] > 0, families, base)

    def both(b, carry):
        for t in range(SLICES):
            combine(t, b)
        return carry

    lax.fori_loop(0, count, both, 0)


def fetch_if(wanted, sources, targets, sems):
    @pl.when(wanted)
    def fetch():
        copies = [
            pltpu.make_async_copy(source, target, sems.at[i])
            for i, (source, target) in enumerate(zip(sources, targets))
        ]
        for copy in copies:
            copy.start()
        for copy in copies:
            copy.wait()


def combine_kernel(start, groups, *refs):
    table, more, refs = refs[:3], refs[3], refs[4:]
    lefts, lates, combined = refs[:groups], refs[groups : 2 * groups], refs[2 * groups]
    held, sems = refs[2 * groups + 1 : -1], refs[-1]
    rows = lefts[0].shape[2]
    sources = [late.at[:, :, pl.ds(start, rows)] for late in lates]
    fetch_if(more[0] > 0, sources, held, sems)
    combine_rows(table, more, lefts, held, combined)


def combine(table, more, lefts, lates, start):
    _, base, rows, width = lefts[0].shape
    families = base + lates[0].shape[1]
    shape = SLICES * len(lefts) * rows, 2 * families * width
    size = shape[0] * shape[1]
    return pl.pallas_call(
        functools.partial(combine_kernel, start, len(lefts)),
        out_shape=jax.ShapeDtypeStruct(shape, jnp.bfloat16),
        in_specs=[spec(pltpu.SMEM)] * 4
        + [spec()] * len(lefts)
        + [spec(pl.ANY)] * len(lates),
        out_specs=spec(),
        scratch_shapes=[pltpu.VMEM((2, families - base, rows, width), jnp.bfloat16)] * len(lates)
        + [pltpu.SemaphoreType.DMA((len(lates),))],
        compiler_params=pltpu.CompilerParams(vmem_limit_bytes=14 << 20),
        cost_estimate=pl.CostEstimate(
            flops=4 * size, transcendentals=0, bytes_accessed=3 * size
        ),
        name="combine",
    )(*table, more, *lefts, *lates)


def product_kernel(groups, chunks, edges, start, halves, more, *refs):
    combined, refs = refs[: len(chunks)], refs[len(chunks) :]
    nears, fars, refs = refs[: len(edges)], refs[len(edges) : 2 * len(edges)], refs[2 * len(edges) :]
    lates, outs, held, sems = refs[:2], refs[2:-3], refs[-3:-1], refs[-1]
    _, width, tile = nears[0].shape
    step = pl.program_id(0)
    columns = pl.ds(pl.multiple_of(start + step * tile, tile), tile)
    fetch_if(more[0] > 0, [late.at[:, :, columns] for late in lates], held, sems)

    def multiply(parts):
        top = 0
        for chunk in combined:
            total, at = None, 0
            for part in parts:
                depth = part.shape[0] * width
                term = jnp.dot(
                    chunk[:, at : at + depth],
                    part[...].reshape(depth, tile),
                    preferred_element_type=jnp.float32,
                )
                total = term if total is None else total + term
                at += depth
            rows = chunk.shape[0] // (SLICES * groups)
            for i in range(SLICES * groups):
                t, group = divmod(i, groups)
                piece = total[i * rows : (i + 1) * rows]
                if halves:
                    out, at = outs[1 - group % 2], group // 2
                else:
                    out, at = outs[group - 1], 0
                out[at, t, top : top + rows] = piece.astype(out.dtype)
            top += rows

    for near, far, (lo, hi) in zip(nears, fars, edges):
        here = (step >= lo) & (step < hi)
        usual = functools.partial(multiply, (near, far))
        full = functools.partial(multiply, (near, far, *held))
        pl.when(here & (more[0] == 0))(usual)
        pl.when(here & (more[0] > 0))(full)


def product(halves, more, combined, nears, fars, lates, start, groups):
    base, width, _ = nears[0].shape
    late = lates[0].shape[0]
    rows = [chunk.shape[0] // (SLICES * groups) for chunk in combined]
    columns = sum(part.shape[2] for part in fars)
    tile = 2 * LANES
    edges, at = [], 0
    for part in fars:
        edges.append((at, at + part.shape[2] // tile))
        at = edges[-1][1]

    def place(lo, hi):
        return lambda i: (0, 0, jnp.clip(i - lo, 0, hi - lo - 1))

    kept, sends = (groups // 2, 1) if halves else (1, groups - 1)
    shape = (kept, SLICES, sum(rows), columns)
    block = pl.BlockSpec((kept, SLICES, sum(rows), tile), lambda i: (0, 0, 0, i))
    return pl.pallas_call(
        functools.partial(product_kernel, groups, rows, edges, start, halves),
        grid=(columns // tile,),
        out_shape=[jax.ShapeDtypeStruct(shape, jnp.bfloat16)] * sends
        + [jax.ShapeDtypeStruct(shape, jnp.float32)],
        in_specs=[spec(pltpu.SMEM)]
        + [
            pl.BlockSpec(chunk.shape, lambda i: (0, 0), pipeline_mode=pl.Buffered(1))
            for chunk in combined
        ]
        + [pl.BlockSpec((base, width, tile), place(lo, hi)) for lo, hi in edges] * 2
        + [spec(pl.ANY)] * 2,
        out_specs=[block] * (sends + 1),
        scratch_shapes=[pltpu.VMEM((late, width, tile), jnp.bfloat16)] * 2
        + [pltpu.SemaphoreType.DMA((2,))],
        compiler_params=pltpu.CompilerParams(vmem_limit_bytes=18 << 20),
        cost_estimate=pl.CostEstimate(
            flops=2 * sum(chunk.size for chunk in combined) * columns,
            transcendentals=0,
            bytes_accessed=sum(2 * chunk.size for chunk in combined)
            + 4 * (base + late) * width * columns,
        ),
        name="product",
    )(more, *combined, *nears, *fars, *lates)


def halve_kernel(keep, came, send, kept):
    for i in range(send.shape[0]):
        kept[i] = keep[2 * i] + came[2 * i].astype(jnp.float32)
        total = keep[2 * i + 1] + came[2 * i + 1].astype(jnp.float32)
        send[i] = total.astype(send.dtype)


def halve(keep, came):
    shape = (keep.shape[0] // 2,) + keep.shape[1:]
    return pl.pallas_call(
        halve_kernel,
        out_shape=(
            jax.ShapeDtypeStruct(shape, jnp.bfloat16),
            jax.ShapeDtypeStruct(shape, jnp.float32),
        ),
        in_specs=[spec()] * 2,
        out_specs=(spec(), spec()),
        cost_estimate=pl.CostEstimate(
            flops=keep.size, transcendentals=0, bytes_accessed=9 * keep.size
        ),
        compiler_params=pltpu.CompilerParams(vmem_limit_bytes=6 << 20),
        name="halve",
    )(keep, came)


def finish_kernel(row, column, count, keep, *refs):
    cames, (out, buffer, sem) = refs[:count], refs[-3:]
    rows, _, columns = buffer.shape
    for t in range(SLICES):
        total = keep[0, t]
        for came in cames:
            total = total + came[0, t].astype(jnp.float32)
        buffer[:, t, :] = total
    target = out.at[pl.ds(row, rows), :, pl.ds(column, columns)]
    copy = pltpu.make_async_copy(buffer, target, sem)
    copy.start()
    copy.wait()


def finish(keep, cames, row, column, rows, order, result):
    here, columns = keep.shape[2:]
    before = [] if result is None else [result]
    return pl.pallas_call(
        functools.partial(finish_kernel, row, column, len(cames)),
        out_shape=jax.ShapeDtypeStruct((rows, SLICES, order), jnp.float32),
        in_specs=[spec()] * (1 + len(cames)) + [spec(pl.ANY)] * len(before),
        out_specs=spec(pl.ANY),
        scratch_shapes=[
            pltpu.VMEM((here, SLICES, columns), jnp.float32),
            pltpu.SemaphoreType.DMA,
        ],
        input_output_aliases={1 + len(cames): 0} if before else {},
        cost_estimate=pl.CostEstimate(
            flops=keep.size, transcendentals=0, bytes_accessed=10 * keep.size
        ),
        compiler_params=pltpu.CompilerParams(vmem_limit_bytes=6 << 20),
        name="finish",
    )(keep, *cames, *before)


def body(blocks, left_ids, right_ids, slice_ids, weight_ids, counts, subduction):
    own = blocks[0]
    families, rows, order = own.shape
    devices = lax.axis_size("pair")
    groups, width = devices // 2, order // devices
    me = lax.axis_index("pair").reshape(1)
    meta = jnp.concatenate([left_ids, right_ids, slice_ids, weight_ids, counts], axis=1)
    metas = lax.all_to_all(
        jnp.broadcast_to(meta, (devices, meta.shape[1])), "pair", 0, 0, tiled=True
    )
    partner = swap(metas, "mom", 1)
    left_order, left_rank, needed, right_rank, more = order_blocks(metas, families)
    right_order = order_blocks(partner, families)[2]
    base = base_count(families)
    row_cuts = cut(rows, SUBLANES, ROW_PARTS)
    column_cuts = cut(order, 2 * LANES, COLUMN_PARTS)
    arrived, nears, fars = [], [], []
    for i, (start, here) in enumerate(row_cuts):
        chosen, number = (left_order, base) if i else (None, families)
        pieces = pack(
            own, chosen, me, 0, number, start, here, width, groups
        )
        moved = [swap(pieces[group], "pair", 2 * group) for group in range(groups - 1, 0, -1)]
        pieces = [pieces[0]] + moved[::-1]
        if not i:
            pieces = list(pick(left_order, base, *pieces))
        arrived.append(pieces)
    for i, (start, columns) in enumerate(column_cuts):
        chosen, number = (right_order, base) if i else (None, families)
        mine = slab(own, chosen, 0, number, start, columns)
        far = swap(mine, ("mom", "pair"), devices + 1)
        near = swap(mine, "mom", 1)
        if not i:
            near, far = pick(needed, base, near[None], far[None])
            near, far = near[0], far[0]
        fars.append(far)
        nears.append(near)
    anywhere = more
    for bit in range(lax.axis_size("mom").bit_length() - 1):
        anywhere = jnp.maximum(anywhere, swap(anywhere, "mom", 1 << bit))
    late_lefts, late_near, late_far = late_blocks(
        own, left_order, right_order, me, anywhere[0] > 0, width, groups
    )
    table = plan(metas, left_rank, right_rank, subduction, families)
    last, columns = len(row_cuts) - 1, range(len(column_cuts))
    jobs = [(range(last), columns[:-1]), (range(last), columns[-1:]), ([last], columns)]
    combined = [
        combine(table, more, lefts, late_lefts, row_cuts[i][0])
        for i, lefts in enumerate(arrived)
    ]
    result = None
    for k, (chunks, parts) in enumerate(jobs):
        row, column = row_cuts[chunks[0]][0], column_cuts[parts[0]][0]
        halves = HALVES[k]
        *sends, keep = functools.partial(product, halves)(
            more,
            [combined[i] for i in chunks],
            [nears[j] for j in parts],
            [fars[j] for j in parts],
            [late_near, late_far],
            column,
            groups,
        )
        apart, steps = 1, [0] * (groups.bit_length() - 2) if halves else []
        for _ in steps:
            came = swap(sends[0], "pair", 2 * apart)
            *sends, keep = halve(keep, came)
            apart *= 2
        if halves:
            cames = [swap(sends[0], "pair", 2 * apart)]
        else:
            cames = [
                swap(sends[group - 1], "pair", 2 * group)
                for group in range(groups - 1, 0, -1)
            ]
        result = finish(keep, cames, row, column, rows, order, result)
    return result.reshape((1,) + result.shape)


def solution(mesh):
    return jax.shard_map(
        body,
        mesh=mesh,
        in_specs=(
            P("mom", None, "pair", None),
            P("mom", "pair"),
            P("mom", "pair"),
            P("mom", "pair"),
            P("mom", "pair"),
            P("mom", "pair"),
            P(),
        ),
        out_specs=P("mom", "pair", None, None),
        check_vma=False,
    )
```
